32 devices in a mesh: sub: 8 (over y, x, core), pole: 4 (over z).
Axes of the slice: x: 2, y: 2, z: 4, core: 2. Of those that a mesh axis runs over, the one named last changes fastest.
Arguments:
- state: float32 [6144, 512], P('sub'), may hold values from -6 to 6
- conductivity: float32 [6144], P('sub'), may hold values from 0.2 to 2
- pole_shift: float32 [4, 2], P('pole'), may hold values from 0.2 to 1
- pole_weight: float32 [4, 2], P('pole'), may hold values from -1.5 to 1.5
- order_list: int32 [8, 1024], P('sub'), may hold values from 0 to 1023, as said below
- inverse: bfloat16 [4, 6144, 2048], P('pole', 'sub'), may hold values from -0.1 to 0.4
Outputs:
- final_state: float32 [6144, 512], P(('sub', 'pole'))
The draws below stay inside these ranges and needn't reach their ends.
Inputs may be any that keep to these rules, and one draw needn't show every extreme that they name: `order_list`: row s holds each of 0 to 1023 exactly once.
All inputs are finite; a program needn't handle non-finite values.
Results may differ from the reference program's by a relative error of at most 0.0052.
Values may be sent and summed in bfloat16 or wider, within the bound.
No kernel may reach another device: no remote copies, remote signals or barrier semaphores. Data moves between devices by JAX's collectives and lax.ppermute only.
A program may use at most 64 MiB of HBM per device.

```python
import math
import jax
import jax.numpy as jnp
from jax import lax

ORDER = 1024
H = 128
SRC = 512
STEPS = 2
SWEEPS = 2
R = 768
SUBS = 8
NROWS = 6144
POLES = 4


def make_orders(key):
    key_list = jax.random.split(jax.random.fold_in(key, 101), SUBS)
    return jax.vmap(lambda sub_key: jax.random.permutation(sub_key, ORDER))(key_list).astype(jnp.int32)


def draw_order_list(key, part):
    return make_orders(key)


def draw_inverse(key, part):
    orders = make_orders(key)
    places = jnp.argsort(orders, axis=1, stable=True).astype(jnp.int32)
    row_ids = jnp.arange(NROWS, dtype=jnp.int32)
    owner = row_ids // R
    local_row = row_ids % R
    column = places[owner, local_row + H]
    first_key, second_key, third_key = jax.random.split(jax.random.fold_in(key, 202), 3)
    columns = jnp.arange(2 * ORDER, dtype=jnp.int32)
    real_mark = (columns[None, :] == column[:, None]).astype(jnp.float32)
    imag_mark = (columns[None, :] == column[:, None] + ORDER).astype(jnp.float32)
    diag_re = 0.2 * jax.random.uniform(first_key, (POLES, NROWS, 1), jnp.float32, 0.6, 1.4)
    diag_im = 0.05 * jax.random.uniform(second_key, (POLES, NROWS, 1), jnp.float32, -1.0, 1.0)
    spread = 0.05 / ORDER ** 0.5
    jitter = spread * jax.random.normal(third_key, (POLES, NROWS, 2 * ORDER), jnp.float32)
    drawn = jitter + diag_re * real_mark[None] + diag_im * imag_mark[None]
    return drawn.astype(jnp.bfloat16)


def steps_of(rng, dims, shards, low, top_value):
    gain = 1.0
    for axis_at, blocks in shards:
        draws = jax.random.uniform(jax.random.fold_in(jax.random.fold_in(rng, 6), axis_at), (blocks,), jnp.float32, low / len(shards), top_value / len(shards))
        gain = gain * jnp.repeat(jnp.exp(draws), dims[axis_at] // blocks).reshape((-1,) + (1,) * (len(dims) - 1 - axis_at))
    return gain


def gaussian(key, shape, scale, bound, cuts=(), kind=jnp.bfloat16):
    loudness = steps_of(key, shape, cuts, -0.22, 0.18) if cuts else 1.0
    values = jax.random.normal(key, shape, jnp.float32) * scale * loudness
    return jnp.minimum(jnp.maximum(values, -bound), bound).astype(kind)


def setup_inputs(seed: int = 0) -> dict:
    streams_of = jax.random.split(jax.random.key(seed), 7)
    return {
        "state": gaussian(streams_of[0], (NROWS, SRC), 1.0, 6.0, ((0, 8),), jnp.float32),
        "conductivity": jnp.clip(jnp.exp(math.log(2.0) - 2.3025851 * jax.random.uniform(streams_of[1], (NROWS,), jnp.float32) ** steps_of(streams_of[1], (NROWS,), ((0, 8),), -0.2, 0.2)), 0.2, 2.0),
        "pole_shift": jnp.clip(0.2 + 0.8 * jax.random.uniform(streams_of[2], (POLES, 2), jnp.float32) ** steps_of(streams_of[2], (POLES, 2), ((0, 4),), -0.2, 0.2), 0.2, 1.0),
        "pole_weight": jnp.clip(jax.random.uniform(streams_of[3], (POLES, 2), jnp.float32, -1.5, 1.5) * steps_of(streams_of[3], (POLES, 2), ((0, 4),), -0.4, 0.0), -1.5, 1.5),
        "order_list": draw_order_list(jax.random.fold_in(streams_of[6], 71), 0),
        "inverse": draw_inverse(jax.random.fold_in(streams_of[6], 71), 0),
    }


def laplace(padded, rim_width):
    inner_count = padded.shape[0] - 2 * rim_width
    middle = padded[rim_width:rim_width + inner_count]
    return (4.0 * middle - padded[rim_width - 1:rim_width - 1 + inner_count]
            - padded[rim_width + 1:rim_width + 1 + inner_count]
            - padded[:inner_count] - padded[2 * rim_width:2 * rim_width + inner_count])


def shifted(padded, sigma_mid, shift_re, shift_im, rim_width):
    laplace_part = laplace(padded, rim_width)
    inner_count = laplace_part.shape[0]
    middle = padded[rim_width:rim_width + inner_count]
    column_half = middle.shape[1] // 2
    real_part = middle[:, :column_half]
    imag_part = middle[:, column_half:]
    sigma_col = sigma_mid[:, None]
    return laplace_part + jnp.concatenate(
        [sigma_col * (shift_re * real_part - shift_im * imag_part),
         sigma_col * (shift_im * real_part + shift_re * imag_part)], axis=1)


def correct(residual_ext, ordering, inverse_block):
    permuted = jnp.take(residual_ext, ordering.astype(jnp.int32), axis=0)
    column_half = permuted.shape[1] // 2
    real_part = permuted[:, :column_half]
    imag_part = permuted[:, column_half:]
    stacked = jnp.concatenate([jnp.concatenate([real_part, imag_part], axis=1),
                               jnp.concatenate([-imag_part, real_part], axis=1)], axis=0)
    return jnp.dot(inverse_block, stacked, preferred_element_type=jnp.float32)


def correct_all(residual, orderings, inverse_pole):
    padded = jnp.pad(residual, ((H, H), (0, 0)))

    def one_block(sub_index):
        extended = lax.dynamic_slice_in_dim(padded, sub_index * R, ORDER, 0)
        ordering = lax.dynamic_index_in_dim(orderings, sub_index, 0, keepdims=False)
        block = lax.dynamic_slice_in_dim(inverse_pole, sub_index * R, R, 0)
        return correct(extended, ordering, block)

    pieces = lax.map(one_block, jnp.arange(SUBS, dtype=jnp.int32))
    return pieces.reshape(NROWS, 2 * SRC)


def reference(state, conductivity, pole_shift, pole_weight, order_list, inverse):
    current = state
    for time_step in range(STEPS):
        right_side = conductivity[:, None] * current
        source = jnp.concatenate([right_side, jnp.zeros_like(right_side)], axis=1)
        summed = jnp.zeros_like(current)
        for pole_index in range(POLES):
            shift_re = pole_shift[pole_index, 0]
            shift_im = pole_shift[pole_index, 1]
            iterate = correct_all(source.astype(jnp.bfloat16), order_list, inverse[pole_index])
            for sweep_index in range(1, SWEEPS):
                padded = jnp.pad(iterate, ((H, H), (0, 0)))
                applied = shifted(padded, conductivity, shift_re, shift_im, H)
                residual = (source - applied).astype(jnp.bfloat16)
                iterate = iterate + correct_all(residual, order_list, inverse[pole_index])
            summed = summed + 2.0 * (pole_weight[pole_index, 0] * iterate[:, :SRC]
                                     - pole_weight[pole_index, 1] * iterate[:, SRC:])
        current = summed
    return current
```

```python
import jax
import jax.numpy as jnp
from jax import lax
from jax.sharding import PartitionSpec as P

STEPS = 2
CHUNKS = 1
BF16 = jnp.bfloat16
F16 = jnp.float16
F32 = jnp.float32


def neighbours(axis):
    count = lax.axis_size(axis)
    up = [(i, i + 1) for i in range(count - 1)]
    return up, [(j, i) for i, j in up]


def partner_of(index, hop, count):
    if count & (count - 1) == 0:
        return index ^ hop, index ^ hop, [(i, i ^ hop) for i in range(count)]
    to = lax.rem(index + hop, count)
    source = lax.rem(index + count - hop, count)
    return to, source, [(i, (i + hop) % count) for i in range(count)]


def natural_order(inverse, ordering):
    width = ordering.shape[0]
    ids = lax.broadcasted_iota(jnp.int32, (width, width), 1)
    place = (ordering[:, None] == ids).astype(BF16)
    real = jnp.dot(inverse[:, :width], place, preferred_element_type=F32).astype(BF16)
    imag = jnp.dot(inverse[:, width:], place, preferred_element_type=F32).astype(BF16)
    return real, imag


def reduce_poles(partial, share):
    count = lax.axis_size("pole")
    index = lax.axis_index("pole")
    columns = partial.shape[1]
    blocks = partial.reshape(count, share, columns)
    top = jnp.max(jnp.abs(blocks), axis=1)
    power = jnp.ceil(jnp.log2(jnp.maximum(top, 1e-30)))
    coded = (blocks * jnp.exp2(12.0 - power)[:, None]).astype(F16)
    tail = jnp.broadcast_to(power.astype(F16)[:, None], (count, 16, columns))
    coded = jnp.concatenate([coded, tail], axis=1)
    total = lax.dynamic_index_in_dim(blocks, index, 0, keepdims=False)
    for hop in range(1, count):
        to, _, pairs = partner_of(index, hop, count)
        sent = lax.dynamic_index_in_dim(coded, to, 0, keepdims=False)
        got = lax.ppermute(sent, "pole", pairs).astype(F32)
        total = total + got[:share] * jnp.exp2(got[share : share + 1] - 12.0)
    return total


def gather_poles(own):
    count = lax.axis_size("pole")
    index = lax.axis_index("pole")
    share = own.shape[0]
    whole = jnp.zeros((count * share, own.shape[1]), own.dtype)
    whole = lax.dynamic_update_slice_in_dim(whole, own, index * share, 0)
    for hop in range(1, count):
        _, source, pairs = partner_of(index, hop, count)
        got = lax.ppermute(own, "pole", pairs)
        whole = lax.dynamic_update_slice_in_dim(whole, got, source * share, 0)
    return whole


def shards(state, conductivity, pole_shift, pole_weight, order_list, inverse):
    rows, columns = state.shape
    rim = (order_list.shape[1] - rows) // 2
    share = rows // lax.axis_size("pole")
    up, down = neighbours("sub")
    g_real, g_imag = natural_order(inverse[0], order_list[0])
    both = jnp.concatenate([g_real, g_imag], axis=0)
    shift_re, shift_im = pole_shift[0, 0], pole_shift[0, 1]
    weight_re, weight_im = pole_weight[0, 0], pole_weight[0, 1]
    sigma = conductivity[:, None]
    sigma_share = lax.dynamic_slice_in_dim(conductivity, lax.axis_index("pole") * share, share, 0)[:, None]

    def sweep(source):
        rounded = source.astype(BF16)
        before = lax.ppermute(rounded[rows - rim :], "sub", up)
        after = lax.ppermute(rounded[:rim], "sub", down)
        first = jnp.dot(both[:, rim : rim + rows], rounded, preferred_element_type=F32)
        first = first + jnp.dot(both[:, :rim], before, preferred_element_type=F32)
        first = first + jnp.dot(both[:, rim + rows :], after, preferred_element_type=F32)
        real, imag = first[:rows], first[rows:]
        source = source.astype(F32)

        def local(x):
            zero = jnp.zeros((rim, x.shape[1]), F32)
            far = jnp.concatenate([zero, x, zero], axis=0)
            near = jnp.pad(x, ((1, 1), (0, 0)))
            return 4.0 * x - near[:rows] - near[2:] - far[:rows] - far[2 * rim :]

        r_real = source - local(real) - sigma * (shift_re * real - shift_im * imag)
        r_imag = -local(imag) - sigma * (shift_im * real + shift_re * imag)
        x = jnp.stack([real, imag])
        r = jnp.stack([r_real, r_imag])
        low = jnp.concatenate([x[:, :rim], r[:, :rim]], axis=0).astype(BF16)
        high = jnp.concatenate([x[:, rows - rim :], r[:, rows - rim :]], axis=0).astype(BF16)
        got_before = lax.ppermute(high, "sub", up).astype(F32)
        got_after = lax.ppermute(low, "sub", down).astype(F32)

        def joined(half):
            mine = x[half]
            xb, qb = got_before[half], got_before[2 + half]
            xa, qa = got_after[half], got_after[2 + half]
            one = lax.broadcasted_iota(jnp.int32, (rim, 1), 0)
            head = r[half, :rim] + xb + jnp.where(one == 0, xb[rim - 1 :], 0.0)
            foot = r[half, rows - rim :] + xa + jnp.where(one == rim - 1, xa[:1], 0.0)
            above = qb + mine[:rim] + jnp.where(one == rim - 1, mine[:1], 0.0)
            below = qa + mine[rows - rim :] + jnp.where(one == 0, mine[rows - 1 :], 0.0)
            return head.astype(BF16), foot.astype(BF16), above, below

        edge = []
        index = lax.axis_index("sub")
        last = lax.axis_size("sub") - 1
        for half in range(2):
            head, foot, above, below = joined(half)
            above = jnp.where(index == 0, 0.0, above).astype(BF16)
            below = jnp.where(index == last, 0.0, below).astype(BF16)
            middle = r[half, rim : rows - rim].astype(BF16)
            edge.append(jnp.concatenate([above, head, middle, foot, below], axis=0))
        e = jnp.concatenate(edge, axis=1)
        n = real.shape[1]
        y = jnp.dot(both, e, preferred_element_type=F32)
        real = real + y[:rows, :n] - y[rows:, n:]
        imag = imag + y[:rows, n:] + y[rows:, :n]
        return 2.0 * (weight_re * real - weight_im * imag)

    results = []
    width = columns // CHUNKS
    for chunk in range(CHUNKS):
        source = sigma * state[:, chunk * width : (chunk + 1) * width]
        for step in range(STEPS):
            total = reduce_poles(sweep(source), share)
            if step + 1 < STEPS:
                source = gather_poles((sigma_share * total).astype(BF16))
        results.append(total)
    return jnp.concatenate(results, axis=1) if CHUNKS > 1 else results[0]


def solution(mesh):
    placed = (
        P("sub", None),
        P("sub"),
        P("pole", None),
        P("pole", None),
        P("sub", None),
        P("pole", "sub", None),
    )
    return jax.shard_map(
        shards, mesh=mesh, in_specs=placed, out_specs=P(("sub", "pole"), None), check_vma=False
    )
```

```python
import functools

import jax
import jax.numpy as jnp
from jax import lax
from jax.experimental import pallas as pl
from jax.experimental.pallas import tpu as pltpu
from jax.sharding import PartitionSpec as P

STEPS = 2
CHUNKS = 1
TAIL = 16
TOP = 12.0
BF16 = jnp.bfloat16
F16 = jnp.float16
F32 = jnp.float32
VMEM = pl.BlockSpec(memory_space=pltpu.VMEM)
SMEM = pl.BlockSpec(memory_space=pltpu.SMEM)


def call(kernel, outs, ins, scratch=(), flops=0, moved=0):
    return pl.pallas_call(
        kernel,
        out_shape=[jax.ShapeDtypeStruct(s, d) for s, d in outs],
        in_specs=[SMEM if s else VMEM for s, _ in ins],
        out_specs=[VMEM] * len(outs),
        scratch_shapes=list(scratch),
        compiler_params=pltpu.CompilerParams(vmem_limit_bytes=30 * 2**20),
        cost_estimate=pl.CostEstimate(flops=flops, bytes_accessed=moved, transcendentals=0),
    )(*[a for _, a in ins])


def dot(a, b):
    return jnp.dot(a, b, preferred_element_type=F32)


def coded(block):
    top = jnp.max(jnp.abs(block), axis=0, keepdims=True)
    power = jnp.ceil(jnp.log2(jnp.maximum(top, 1e-30)))
    return block * jnp.exp2(TOP - power), jnp.broadcast_to(power, (TAIL, block.shape[1]))


def pick(flag, a, b):
    return jnp.where(flag == 0, a, b)


def order_kernel(order_ref, inv_ref, g_ref):
    rows, width = inv_ref.shape[0], inv_ref.shape[1] // 2
    ids = lax.broadcasted_iota(jnp.int32, (width, width), 1)
    place = (order_ref[...] == ids).astype(BF16)
    g_ref[:rows] = dot(inv_ref[:, :width], place).astype(BF16)
    g_ref[rows:] = dot(inv_ref[:, width:], place).astype(BF16)


def first_kernel(rim, scaled, shift_ref, weight_ref, ids_ref, g_ref, src_ref, one_ref, two_ref, sigma_ref,
                 base_ref, mid_ref, edge_ref, msg1_ref, msg2_ref, e_ref, xr_ref, xi_ref):
    rows, n = src_ref.shape
    parity = ids_ref[0, 0]
    e_ref[:rim] = pick(parity, two_ref[...], one_ref[...])
    e_ref[rim + rows:] = pick(parity, one_ref[...], two_ref[...])
    if scaled:
        e_ref[rim:rim + rows] = (src_ref[...] * sigma_ref[...]).astype(BF16)
    else:
        e_ref[rim:rim + rows] = src_ref[...]
    for ref, lo in ((xr_ref, 0), (xi_ref, rows)):
        ref[:8] = jnp.zeros((8, n), F32)
        ref[8 + rows:] = jnp.zeros((8, n), F32)
        ref[8:8 + rows] = dot(g_ref[lo:lo + rows], e_ref[...])
    a, b = shift_ref[0, 0], shift_ref[0, 1]
    wr, wi = 2.0 * weight_ref[0, 0], 2.0 * weight_ref[0, 1]
    step = 32

    def local(ref, lo):
        mid = 4.0 * ref[8 + lo:8 + lo + step] - ref[7 + lo:7 + lo + step] - ref[9 + lo:9 + lo + step]
        if lo >= rim:
            mid = mid - ref[8 + lo - rim:8 + lo - rim + step]
        if lo + rim < rows:
            mid = mid - ref[8 + lo + rim:8 + lo + rim + step]
        return mid

    for lo in range(0, rows, step):
        at = slice(lo, lo + step)
        xr, xi = xr_ref[8 + lo:8 + lo + step], xi_ref[8 + lo:8 + lo + step]
        sigma = sigma_ref[at]
        source = src_ref[at] * sigma if scaled else src_ref[at].astype(F32)
        rr = source - local(xr_ref, lo) - sigma * (a * xr - b * xi)
        ri = -local(xi_ref, lo) - sigma * (b * xr + a * xi)
        base_ref[at] = wr * xr - wi * xi
        if lo < rim or lo >= rows - rim:
            side, row = (0, lo) if lo < rim else (1, lo - rows + rim)
            for k, v in enumerate((xr, xi, rr, ri)):
                edge_ref[side, k * rim + row:k * rim + row + step] = v
        else:
            mid_ref[0, lo - rim:lo - rim + step] = rr.astype(BF16)
            mid_ref[1, lo - rim:lo - rim + step] = ri.astype(BF16)
    low, low_tail = coded(edge_ref[0])
    high, high_tail = coded(edge_ref[1])
    msg1_ref[:4 * rim] = pick(parity, high, low)
    msg2_ref[:4 * rim] = pick(parity, low, high)
    msg1_ref[4 * rim:] = pick(parity, high_tail, low_tail)
    msg2_ref[4 * rim:] = pick(parity, low_tail, high_tail)


def product(g_ref, rows, cols, er, ei, wr, wi):
    gr, gi = g_ref[:rows, cols], g_ref[rows:, cols]
    return wr * (dot(gr, er) - dot(gi, ei)) - wi * (dot(gr, ei) + dot(gi, er))


def middle_kernel(rim, weight_ref, g_ref, base_ref, mid_ref, out_ref):
    rows = base_ref.shape[0]
    wr, wi = 2.0 * weight_ref[0, 0], 2.0 * weight_ref[0, 1]
    out_ref[...] = base_ref[...] + product(g_ref, rows, slice(2 * rim, rows), mid_ref[0], mid_ref[1], wr, wi)


def last_kernel(rim, hops, weight_ref, ids_ref, g_ref, part_ref, edge_ref, one_ref, two_ref, *rest):
    own_ref, msgs, u_ref, e_ref = rest[0], rest[1:1 + hops], rest[1 + hops], rest[2 + hops]
    rows, n = part_ref.shape
    share = own_ref.shape[0]
    parity, first, final = ids_ref[0, 0], ids_ref[0, 1], ids_ref[0, 2]
    wr, wi = 2.0 * weight_ref[0, 0], 2.0 * weight_ref[0, 1]
    before = pick(parity, two_ref[...], one_ref[...])
    after = pick(parity, one_ref[...], two_ref[...])
    before = before[:4 * rim] * jnp.exp2(before[4 * rim:4 * rim + 1] - TOP)
    after = after[:4 * rim] * jnp.exp2(after[4 * rim:4 * rim + 1] - TOP)
    at = lax.broadcasted_iota(jnp.int32, (rim, 1), 0)
    for half in range(2):
        x, r = slice(half * rim, (half + 1) * rim), slice((2 + half) * rim, (3 + half) * rim)
        xb, qb, xa, qa = before[x], before[r], after[x], after[r]
        low, high = edge_ref[0, x], edge_ref[1, x]
        above = qb + low + jnp.where(at == rim - 1, low[:1], 0.0)
        below = qa + high + jnp.where(at == 0, high[rim - 1:], 0.0)
        head = edge_ref[0, r] + xb + jnp.where(at == 0, xb[rim - 1:], 0.0)
        foot = edge_ref[1, r] + xa + jnp.where(at == rim - 1, xa[:1], 0.0)
        e_ref[half, :rim] = jnp.where(first == 1, 0.0, above).astype(BF16)
        e_ref[half, rim:2 * rim] = head.astype(BF16)
        e_ref[half, 2 * rim:3 * rim] = foot.astype(BF16)
        e_ref[half, 3 * rim:] = jnp.where(final == 1, 0.0, below).astype(BF16)
    u_ref[...] = part_ref[...] + product(
        g_ref, rows, slice(0, 2 * rim), e_ref[0, :2 * rim], e_ref[1, :2 * rim], wr, wi
    ) + product(
        g_ref, rows, slice(rows, rows + 2 * rim), e_ref[0, 2 * rim:], e_ref[1, 2 * rim:], wr, wi
    )
    own_ref[...] = u_ref[pl.ds(pl.multiple_of(ids_ref[0, 3] * share, share), share)]
    for hop, ref in enumerate(msgs):
        block = u_ref[pl.ds(pl.multiple_of(ids_ref[0, 4 + hop] * share, share), share)]
        ref[:share], ref[share:] = coded(block)


def join_kernel(rim, ids_ref, own_ref, *rest):
    got, (src_ref, msg1_ref, msg2_ref) = rest[:-3], rest[-3:]
    share = own_ref.shape[0]
    rows = src_ref.shape[0]
    parity = ids_ref[0, 0]
    for k, ref in enumerate((own_ref,) + tuple(got)):
        src_ref[pl.ds(pl.multiple_of(ids_ref[0, 3 + k] * share, share), share)] = ref[...]
    low, high = src_ref[:rim], src_ref[rows - rim:]
    msg1_ref[...] = pick(parity, high, low)
    msg2_ref[...] = pick(parity, low, high)


def shards(state, conductivity, pole_shift, pole_weight, order_list, inverse):
    rows, columns = state.shape
    order = order_list.shape[1]
    rim = (order - rows) // 2
    subs, poles = lax.axis_size("sub"), lax.axis_size("pole")
    sub, pole = lax.axis_index("sub"), lax.axis_index("pole")
    share, hops = rows // poles, poles - 1
    n = columns // CHUNKS
    pairs1 = [(i ^ 1, i) for i in range(subs) if i ^ 1 < subs]
    pairs2 = [(j, i) for i in range(subs) for j in [((i + 1) ^ 1) - 1] if 0 <= j < subs]
    if poles & hops == 0:
        target = [pole ^ k for k in range(1, poles)]
        source_of = target
        hop_pairs = [[(i, i ^ k) for i in range(poles)] for k in range(1, poles)]
    else:
        target = [lax.rem(pole + k, poles) for k in range(1, poles)]
        source_of = [lax.rem(pole + poles - k, poles) for k in range(1, poles)]
        hop_pairs = [[(i, (i + k) % poles) for i in range(poles)] for k in range(1, poles)]
    flags = [sub % 2, (sub == 0).astype(jnp.int32), (sub == subs - 1).astype(jnp.int32), pole]
    to_ids = jnp.stack([f.astype(jnp.int32) for f in flags + target])[None]
    from_ids = to_ids if source_of is target else jnp.stack([f.astype(jnp.int32) for f in flags + source_of])[None]
    parity = sub % 2
    sigma = conductivity[:, None]
    sigma_share = lax.dynamic_slice_in_dim(conductivity, pole * share, share, 0)[:, None]

    (g,) = call(
        order_kernel, [((2 * rows, order), BF16)], [(0, order_list.reshape(order, 1)), (0, inverse[0])],
        flops=4 * rows * order * order, moved=6 * rows * order,
    )

    def exchange(one, two):
        return lax.ppermute(one, "sub", pairs1), lax.ppermute(two, "sub", pairs2)

    def sweep(source, got, scaled):
        base, mid, edge, msg1, msg2 = call(
            functools.partial(first_kernel, rim, scaled),
            [((rows, n), F32), ((2, rows - 2 * rim, n), BF16), ((2, 4 * rim, n), F32),
             ((4 * rim + TAIL, n), F32), ((4 * rim + TAIL, n), F32)],
            [(1, pole_shift), (1, pole_weight), (1, to_ids), (0, g), (0, source), (0, got[0]), (0, got[1]), (0, sigma)],
            [pltpu.VMEM((order, n), BF16), pltpu.VMEM((rows + 16, n), F32), pltpu.VMEM((rows + 16, n), F32)],
            flops=4 * rows * order * n, moved=4 * rows * order,
        )
        got = exchange(msg1.astype(F16), msg2.astype(F16))
        (part,) = call(
            functools.partial(middle_kernel, rim), [((rows, n), F32)],
            [(1, pole_weight), (0, g), (0, base), (0, mid)],
            flops=8 * rows * (rows - 2 * rim) * n, moved=4 * rows * order,
        )
        return call(
            functools.partial(last_kernel, rim, hops), [((share, n), F32)] + [((share + TAIL, n), F32)] * hops,
            [(1, pole_weight), (1, to_ids), (0, g), (0, part), (0, edge), (0, got[0].astype(F32)), (0, got[1].astype(F32))],
            [pltpu.VMEM((rows, n), F32), pltpu.VMEM((2, 4 * rim, n), BF16)],
            flops=8 * rows * 4 * rim * n, moved=4 * rows * order,
        )

    def reduced(own, *sent):
        for block, pairs in zip(sent, hop_pairs):
            got = lax.ppermute(block.astype(F16), "pole", pairs).astype(F32)
            own = own + got[:share] * jnp.exp2(got[share:share + 1] - TOP)
        return own

    def gathered(own):
        got = [lax.ppermute(own, "pole", pairs) for pairs in hop_pairs]
        return call(
            functools.partial(join_kernel, rim), [((rows, n), BF16), ((rim, n), BF16), ((rim, n), BF16)],
            [(1, from_ids), (0, own)] + [(0, x) for x in got], moved=4 * rows * n,
        )

    results = []
    for chunk in range(CHUNKS):
        source = state[:, chunk * n:(chunk + 1) * n]
        low = (sigma[:rim] * source[:rim]).astype(BF16)
        high = (sigma[rows - rim:] * source[rows - rim:]).astype(BF16)
        one, two = pick(parity, high, low), pick(parity, low, high)
        for step in range(STEPS):
            total = reduced(*sweep(source, exchange(one, two), step == 0))
            if step + 1 < STEPS:
                source, one, two = gathered((sigma_share * total).astype(BF16))
        results.append(total)
    return jnp.concatenate(results, axis=1) if CHUNKS > 1 else results[0]


def solution(mesh):
    placed = (
        P("sub", None),
        P("sub"),
        P("pole", None),
        P("pole", None),
        P("sub", None),
        P("pole", "sub", None),
    )
    return jax.shard_map(
        shards, mesh=mesh, in_specs=placed, out_specs=P(("sub", "pole"), None), check_vma=False
    )
```

```python
import functools

import jax
import jax.numpy as jnp
from jax import lax
from jax.experimental import pallas as pl
from jax.experimental.pallas import tpu as pltpu
from jax.sharding import PartitionSpec as P

STEPS = 2
CHUNKS = 2
TAIL = 8
TOP = 12.0
BF16 = jnp.bfloat16
F16 = jnp.float16
F32 = jnp.float32
VMEM = pl.BlockSpec(memory_space=pltpu.VMEM)
SMEM = pl.BlockSpec(memory_space=pltpu.SMEM)
HBM = pl.BlockSpec(memory_space=pltpu.HBM)


def call(kernel, outs, ins, scratch=(), flops=0, moved=0):
    return pl.pallas_call(
        kernel,
        out_shape=[jax.ShapeDtypeStruct(s, d) for s, d in outs],
        in_specs=[s for s, _ in ins],
        out_specs=[VMEM] * len(outs),
        scratch_shapes=list(scratch),
        compiler_params=pltpu.CompilerParams(vmem_limit_bytes=16 * 2**20),
        cost_estimate=pl.CostEstimate(flops=flops, bytes_accessed=moved, transcendentals=0),
    )(*[a for _, a in ins])


def dot(a, b):
    return jnp.dot(a, b, preferred_element_type=F32)


def coded(block):
    top = jnp.max(jnp.abs(block), axis=0, keepdims=True)
    power = jnp.ceil(jnp.log2(jnp.maximum(top, 1e-30)))
    return block * jnp.exp2(TOP - power), jnp.broadcast_to(power, (TAIL, block.shape[1]))


def pick(flag, a, b):
    return jnp.where(flag == 0, a, b)


def hop_target(pole, hop, poles):
    return pole ^ hop if poles & (poles - 1) == 0 else lax.rem(pole + hop, poles)


def hop_source(pole, hop, poles):
    return pole ^ hop if poles & (poles - 1) == 0 else lax.rem(pole + poles - hop, poles)


def hop_pairs(hop, poles):
    return [(i, i ^ hop if poles & (poles - 1) == 0 else (i + hop) % poles) for i in range(poles)]


def rows_of(index, share):
    return pl.ds(pl.multiple_of(index * share, share), share)


def column(row, count):
    return jnp.transpose(jnp.broadcast_to(row, (8, count)))[:, :1]


def start_kernel(sigma_ref, state_hbm, msg1_ref, msg2_ref, wide_ref, low_ref, high_ref, low_sem, high_sem):
    rows, rim = state_hbm.shape[0], low_ref.shape[0]
    low_copy = pltpu.make_async_copy(state_hbm.at[pl.ds(0, rim)], low_ref, low_sem)
    high_copy = pltpu.make_async_copy(state_hbm.at[pl.ds(rows - rim, rim)], high_ref, high_sem)
    low_copy.start()
    high_copy.start()
    sigma = column(sigma_ref[...], rows)
    wide_ref[...] = jnp.broadcast_to(sigma, wide_ref.shape)
    parity = lax.rem(lax.axis_index("sub"), 2)
    low_copy.wait()
    high_copy.wait()
    low = (low_ref[...] * sigma[:rim]).astype(BF16)
    high = (high_ref[...] * sigma[rows - rim:]).astype(BF16)
    msg1_ref[...] = pick(parity, high, low)
    msg2_ref[...] = pick(parity, low, high)


def setup_kernel(order_ref, wide_ref, inv_hbm, state_hbm, g_ref, share_ref, *rest):
    chunks, (inv_ref, state_ref, inv_sem, state_sem) = rest[:-4], rest[-4:]
    rows, width = inv_ref.shape[0], inv_ref.shape[1] // 2
    n, share = share_ref.shape[1], share_ref.shape[0]
    inv_copy = pltpu.make_async_copy(inv_hbm.at[0], inv_ref, inv_sem)
    state_copy = pltpu.make_async_copy(state_hbm, state_ref, state_sem)
    inv_copy.start()
    state_copy.start()
    share_ref[...] = wide_ref[rows_of(lax.axis_index("pole"), share)]
    order = column(order_ref[...].astype(F32), width).astype(jnp.int32)
    ids = lax.broadcasted_iota(jnp.int32, (width, width), 1)
    place = (order == ids).astype(BF16)
    inv_copy.wait()
    g_ref[:rows] = dot(inv_ref[:, :width], place).astype(BF16)
    g_ref[rows:] = dot(inv_ref[:, width:], place).astype(BF16)
    state_copy.wait()
    for k, ref in enumerate(chunks):
        ref[...] = state_ref[:, k * n:(k + 1) * n] * wide_ref[...]


def stencil(ref, lo, count, rim, far_up, far_down):
    mid = 4.0 * ref[8 + lo:8 + lo + count] - ref[7 + lo:7 + lo + count] - ref[9 + lo:9 + lo + count]
    if far_up:
        mid = mid - ref[8 + lo - rim:8 + lo - rim + count]
    if far_down:
        mid = mid - ref[8 + lo + rim:8 + lo + rim + count]
    return mid


def residual(xr_ref, xi_ref, at, lo, count, rim, far_up, far_down, src_ref, sigma_ref, a, b):
    xr, xi = xr_ref[8 + lo:8 + lo + count], xi_ref[8 + lo:8 + lo + count]
    sigma = sigma_ref[at]
    rr = src_ref[at].astype(F32) - stencil(xr_ref, lo, count, rim, far_up, far_down) - sigma * (a * xr - b * xi)
    ri = -stencil(xi_ref, lo, count, rim, far_up, far_down) - sigma * (b * xr + a * xi)
    return xr, xi, rr, ri


def edge_kernel(rim, lane, shift_ref, g_ref, src_ref, one_ref, two_ref, sigma_ref,
                ext_ref, x_ref, edge_ref, msg1_ref, msg2_ref, xr_ref, xi_ref):
    rows, n = src_ref.shape
    parity = lax.rem(lax.axis_index("sub"), 2)
    one, two = one_ref[:, lane:lane + n], two_ref[:, lane:lane + n]
    ext_ref[:rim] = pick(parity, two, one)
    ext_ref[rim:rim + rows] = src_ref[...].astype(BF16)
    ext_ref[rim + rows:] = pick(parity, one, two)
    a, b = shift_ref[0, 0], shift_ref[0, 1]
    span, step = 2 * rim, 32
    for side in range(2):
        lo = side * (rows - span)
        for half, ref in ((0, xr_ref), (1, xi_ref)):
            ref[:8] = jnp.zeros((8, n), F32)
            ref[8 + span:] = jnp.zeros((8, n), F32)
            block = dot(g_ref[half * rows + lo:half * rows + lo + span], ext_ref[...])
            ref[8:8 + span] = block
            x_ref[side, half] = block
        for k in range(0, rim, step):
            at = side * rim + k
            out = residual(xr_ref, xi_ref, slice(lo + at, lo + at + step), at, step, rim, side == 1, side == 0,
                           src_ref, sigma_ref, a, b)
            for j, v in enumerate(out):
                edge_ref[side, j * rim + k:j * rim + k + step] = v
    low, low_tail = coded(edge_ref[0])
    high, high_tail = coded(edge_ref[1])
    msg1_ref[:4 * rim] = pick(parity, high, low)
    msg2_ref[:4 * rim] = pick(parity, low, high)
    msg1_ref[4 * rim:] = pick(parity, high_tail, low_tail)
    msg2_ref[4 * rim:] = pick(parity, low_tail, high_tail)


def product(g_ref, rows, cols, er, ei, wr, wi):
    gr, gi = g_ref[:rows, cols], g_ref[rows:, cols]
    return wr * (dot(gr, er) - dot(gi, ei)) - wi * (dot(gr, ei) + dot(gi, er))


def middle_kernel(rim, shift_ref, weight_ref, g_ref, src_ref, ext_ref, x_ref, sigma_ref, out_ref, xr_ref, xi_ref, e_ref):
    rows, n = src_ref.shape
    span = 2 * rim
    a, b = shift_ref[0, 0], shift_ref[0, 1]
    wr, wi = 2.0 * weight_ref[0, 0], 2.0 * weight_ref[0, 1]
    for half, ref in ((0, xr_ref), (1, xi_ref)):
        ref[8:8 + span] = x_ref[0, half]
        ref[8 + rows - span:8 + rows] = x_ref[1, half]
        if rows > 2 * span:
            ref[8 + span:8 + rows - span] = dot(g_ref[half * rows + span:half * rows + rows - span], ext_ref[...])
    step = 32
    for lo in range(0, rows, step):
        at = slice(lo, lo + step)
        if rim <= lo < rows - rim:
            xr, xi, rr, ri = residual(xr_ref, xi_ref, at, lo, step, rim, True, True, src_ref, sigma_ref, a, b)
            e_ref[0, lo - rim:lo - rim + step] = rr.astype(BF16)
            e_ref[1, lo - rim:lo - rim + step] = ri.astype(BF16)
    base = wr * xr_ref[8:8 + rows] - wi * xi_ref[8:8 + rows]
    out_ref[...] = base + product(g_ref, rows, slice(span, rows), e_ref[0], e_ref[1], wr, wi)


def last_kernel(rim, hops, weight_ref, g_ref, part_ref, edge_ref, one_ref, two_ref, *rest):
    own_ref, msgs, u_ref, e_ref = rest[0], rest[1:1 + hops], rest[1 + hops], rest[2 + hops]
    rows, n = part_ref.shape
    share = own_ref.shape[0]
    sub, pole = lax.axis_index("sub"), lax.axis_index("pole")
    parity, first, final = lax.rem(sub, 2), sub == 0, sub == lax.axis_size("sub") - 1
    wr, wi = 2.0 * weight_ref[0, 0], 2.0 * weight_ref[0, 1]
    before = pick(parity, two_ref[...], one_ref[...])
    after = pick(parity, one_ref[...], two_ref[...])
    before = before[:4 * rim] * jnp.exp2(before[4 * rim:4 * rim + 1] - TOP)
    after = after[:4 * rim] * jnp.exp2(after[4 * rim:4 * rim + 1] - TOP)
    at = lax.broadcasted_iota(jnp.int32, (rim, 1), 0)
    for half in range(2):
        x, r = slice(half * rim, (half + 1) * rim), slice((2 + half) * rim, (3 + half) * rim)
        xb, qb, xa, qa = before[x], before[r], after[x], after[r]
        low, high = edge_ref[0, x], edge_ref[1, x]
        above = qb + low + jnp.where(at == rim - 1, low[:1], 0.0)
        below = qa + high + jnp.where(at == 0, high[rim - 1:], 0.0)
        head = edge_ref[0, r] + xb + jnp.where(at == 0, xb[rim - 1:], 0.0)
        foot = edge_ref[1, r] + xa + jnp.where(at == rim - 1, xa[:1], 0.0)
        e_ref[half, :rim] = jnp.where(first, 0.0, above).astype(BF16)
        e_ref[half, rim:2 * rim] = head.astype(BF16)
        e_ref[half, 2 * rim:3 * rim] = foot.astype(BF16)
        e_ref[half, 3 * rim:] = jnp.where(final, 0.0, below).astype(BF16)
    u_ref[...] = part_ref[...] + product(
        g_ref, rows, slice(0, 2 * rim), e_ref[0, :2 * rim], e_ref[1, :2 * rim], wr, wi
    ) + product(
        g_ref, rows, slice(rows, rows + 2 * rim), e_ref[0, 2 * rim:], e_ref[1, 2 * rim:], wr, wi
    )
    own_ref[...] = u_ref[rows_of(pole, share)]
    for hop, ref in enumerate(msgs):
        ref[:share], ref[share:] = coded(u_ref[rows_of(hop_target(pole, hop + 1, hops + 1), share)])


def join_kernel(rim, own_ref, *rest):
    got, (src_ref, msg1_ref, msg2_ref) = rest[:-3], rest[-3:]
    share, rows, poles = own_ref.shape[0], src_ref.shape[0], len(got) + 1
    parity, pole = lax.rem(lax.axis_index("sub"), 2), lax.axis_index("pole")
    src_ref[rows_of(pole, share)] = own_ref[...]
    for hop, ref in enumerate(got):
        src_ref[rows_of(hop_source(pole, hop + 1, poles), share)] = ref[...]
    low, high = src_ref[:rim], src_ref[rows - rim:]
    msg1_ref[...] = pick(parity, high, low)
    msg2_ref[...] = pick(parity, low, high)


def shards(state, conductivity, pole_shift, pole_weight, order_list, inverse):
    rows, columns = state.shape
    order = order_list.shape[1]
    rim = (order - rows) // 2
    subs, poles = lax.axis_size("sub"), lax.axis_size("pole")
    share, hops = rows // poles, poles - 1
    n = columns // CHUNKS
    pairs1 = [(i ^ 1, i) for i in range(subs) if i ^ 1 < subs]
    pairs2 = [(j, i) for i in range(subs) for j in [((i + 1) ^ 1) - 1] if 0 <= j < subs]
    def exchange(one, two):
        return lax.ppermute(one, "sub", pairs1), lax.ppermute(two, "sub", pairs2)

    one, two, sigma = call(
        start_kernel, [((rim, columns), BF16), ((rim, columns), BF16), ((rows, n), F32)],
        [(VMEM, conductivity.reshape(1, rows)), (HBM, state)],
        [pltpu.VMEM((rim, columns), F32), pltpu.VMEM((rim, columns), F32),
         pltpu.SemaphoreType.DMA, pltpu.SemaphoreType.DMA],
        moved=8 * rim * columns,
    )
    first_halo = exchange(one, two)
    g, sigma_share, *sources = call(
        setup_kernel, [((2 * rows, order), BF16), ((share, n), F32)] + [((rows, n), F32)] * CHUNKS,
        [(VMEM, order_list), (VMEM, sigma), (HBM, inverse), (HBM, state)],
        [pltpu.VMEM((rows, 2 * order), BF16), pltpu.VMEM((rows, columns), F32),
         pltpu.SemaphoreType.DMA, pltpu.SemaphoreType.DMA],
        flops=4 * rows * order * order, moved=6 * rows * order,
    )

    def sweep(source, got, lane):
        ext, x, edge, msg1, msg2 = call(
            functools.partial(edge_kernel, rim, lane),
            [((order, n), BF16), ((2, 2, 2 * rim, n), F32), ((2, 4 * rim, n), F32),
             ((4 * rim + TAIL, n), F32), ((4 * rim + TAIL, n), F32)],
            [(SMEM, pole_shift), (VMEM, g), (VMEM, source), (VMEM, got[0]), (VMEM, got[1]), (VMEM, sigma)],
            [pltpu.VMEM((2 * rim + 16, n), F32), pltpu.VMEM((2 * rim + 16, n), F32)],
            flops=16 * rim * order * n, moved=4 * rows * order,
        )
        got = exchange(msg1.astype(F16), msg2.astype(F16))
        (part,) = call(
            functools.partial(middle_kernel, rim), [((rows, n), F32)],
            [(SMEM, pole_shift), (SMEM, pole_weight), (VMEM, g), (VMEM, source), (VMEM, ext), (VMEM, x), (VMEM, sigma)],
            [pltpu.VMEM((rows + 16, n), F32), pltpu.VMEM((rows + 16, n), F32), pltpu.VMEM((2, rows - 2 * rim, n), BF16)],
            flops=8 * rows * rows * n, moved=4 * rows * order,
        )
        return call(
            functools.partial(last_kernel, rim, hops), [((share, n), F32)] + [((share + TAIL, n), F32)] * hops,
            [(SMEM, pole_weight), (VMEM, g), (VMEM, part), (VMEM, edge), (VMEM, got[0].astype(F32)), (VMEM, got[1].astype(F32))],
            [pltpu.VMEM((rows, n), F32), pltpu.VMEM((2, 4 * rim, n), BF16)],
            flops=8 * rows * 4 * rim * n, moved=4 * rows * order,
        )

    def reduced(own, *sent):
        for hop, block in enumerate(sent):
            got = lax.ppermute(block.astype(F16), "pole", hop_pairs(hop + 1, poles)).astype(F32)
            own = own + got[:share] * jnp.exp2(got[share:share + 1] - TOP)
        return own

    def gathered(own):
        got = [lax.ppermute(own, "pole", hop_pairs(hop, poles)) for hop in range(1, poles)]
        return call(
            functools.partial(join_kernel, rim), [((rows, n), BF16), ((rim, n), BF16), ((rim, n), BF16)],
            [(VMEM, own)] + [(VMEM, x) for x in got], moved=4 * rows * n,
        )

    results = []
    for chunk in range(CHUNKS):
        source, halo = sources[chunk], first_halo
        for step in range(STEPS):
            total = reduced(*sweep(source, halo, 0 if step else chunk * n))
            if step + 1 < STEPS:
                source, one, two = gathered((sigma_share * total).astype(BF16))
                halo = exchange(one, two)
        results.append(total)
    return jnp.concatenate(results, axis=1) if CHUNKS > 1 else results[0]


def solution(mesh):
    placed = (
        P("sub", None),
        P("sub"),
        P("pole", None),
        P("pole", None),
        P("sub", None),
        P("pole", "sub", None),
    )
    return jax.shard_map(
        shards, mesh=mesh, in_specs=placed, out_specs=P(("sub", "pole"), None), check_vma=False
    )
```

```python
import functools

import jax
import jax.numpy as jnp
from jax import lax
from jax.experimental import pallas as pl
from jax.experimental.pallas import tpu as pltpu
from jax.sharding import PartitionSpec as P


STEPS = 2
CHUNKS = 2
TAIL = 8
TOP = 12.0
BF16 = jnp.bfloat16
F16 = jnp.float16
F32 = jnp.float32
VMEM = pl.BlockSpec(memory_space=pltpu.VMEM)
SMEM = pl.BlockSpec(memory_space=pltpu.SMEM)


def call(kernel, outs, ins, scratch=(), flops=0, moved=0, alias=()):
    return pl.pallas_call(
        kernel,
        out_shape=[jax.ShapeDtypeStruct(s, d) for s, d in outs],
        in_specs=[s for s, _ in ins],
        out_specs=[VMEM] * len(outs),
        scratch_shapes=list(scratch),
        input_output_aliases=dict(alias),
        compiler_params=pltpu.CompilerParams(vmem_limit_bytes=16 * 2**20),
        cost_estimate=pl.CostEstimate(flops=flops, bytes_accessed=moved, transcendentals=0),
    )(*[a for _, a in ins])


def dot(a, b):
    return jnp.dot(a, b, preferred_element_type=F32)


def store_coded(ref, blocks):
    top = functools.reduce(jnp.maximum, [jnp.max(jnp.abs(b), axis=0, keepdims=True) for b in blocks])
    power = jnp.ceil(jnp.log2(jnp.maximum(top, 1e-30)))
    scale, at = jnp.exp2(TOP - power), 0
    for block in blocks:
        ref[at:at + block.shape[0]] = block * scale
        at += block.shape[0]
    ref[at:] = jnp.broadcast_to(power, (TAIL, top.shape[1]))


def pick(flag, a, b):
    return jnp.where(flag == 0, a, b)


def hop_target(pole, hop, poles):
    return pole ^ hop if poles & (poles - 1) == 0 else lax.rem(pole + hop, poles)


def hop_source(pole, hop, poles):
    return pole ^ hop if poles & (poles - 1) == 0 else lax.rem(pole + poles - hop, poles)


def hop_pairs(hop, poles):
    return [(i, i ^ hop if poles & (poles - 1) == 0 else (i + hop) % poles) for i in range(poles)]


def rows_of(index, share):
    return pl.ds(pl.multiple_of(index * share, share), share)


def column(row, count):
    return jnp.transpose(jnp.broadcast_to(row, (8, count)))[:, :1]


def start_kernel(rim, sigma_ref, order_ref, state_ref, msg1_ref, msg2_ref, wide_ref, share_ref, row_ref, *chunks):
    rows, n, share = state_ref.shape[0], wide_ref.shape[1], share_ref.shape[0]
    parity = lax.rem(lax.axis_index("sub"), 2)
    sigma = column(sigma_ref[...].reshape(1, rows), rows)
    low = (state_ref[:rim] * sigma[:rim]).astype(BF16)
    high = (state_ref[rows - rim:] * sigma[rows - rim:]).astype(BF16)
    msg1_ref[...] = pick(parity, high, low)
    msg2_ref[...] = pick(parity, low, high)
    wide_ref[...] = jnp.broadcast_to(sigma, wide_ref.shape)
    share_ref[...] = wide_ref[rows_of(lax.axis_index("pole"), share)]
    row_ref[...] = order_ref[...].astype(F32)
    for k, ref in enumerate(chunks):
        ref[...] = state_ref[:, k * n:(k + 1) * n] * sigma


def setup_kernel(row_ref, inv_ref, g_ref):
    rows, width = inv_ref.shape[1], inv_ref.shape[2] // 2
    ids = lax.broadcasted_iota(jnp.int32, (width, width), 1)
    place = (column(row_ref[...], width).astype(jnp.int32) == ids).astype(BF16)
    g_ref[:rows] = dot(inv_ref[0, :, :width], place).astype(BF16)
    g_ref[rows:] = dot(inv_ref[0, :, width:], place).astype(BF16)


def stencil(x_ref, half, lo, count, rim, far_up, far_down):
    def row(shift):
        return x_ref[half, 8 + lo + shift:8 + lo + shift + count]

    mid = 4.0 * row(0) - row(-1) - row(1)
    if far_up:
        mid = mid - row(-rim)
    if far_down:
        mid = mid - row(rim)
    return mid


def residual(x_ref, lo, count, rim, far_up, far_down, src_ref, sigma_ref, a, b):
    at = slice(lo, lo + count)
    xr, xi, sigma = x_ref[0, 8 + lo:8 + lo + count], x_ref[1, 8 + lo:8 + lo + count], sigma_ref[at]
    real = src_ref[at].astype(F32) - stencil(x_ref, 0, lo, count, rim, far_up, far_down) - sigma * (a * xr - b * xi)
    imag = -stencil(x_ref, 1, lo, count, rim, far_up, far_down) - sigma * (b * xr + a * xi)
    return real, imag


def edge_kernel(rim, lane, shift_ref, g_ref, src_ref, one_ref, two_ref, sigma_ref, ext_ref, x_ref, r_ref, msgs_ref):
    rows, n = src_ref.shape
    parity = lax.rem(lax.axis_index("sub"), 2)
    one, two = one_ref[:, lane:lane + n], two_ref[:, lane:lane + n]
    ext_ref[:rim] = pick(parity, two, one)
    ext_ref[rim:rim + rows] = src_ref[...].astype(BF16)
    ext_ref[rim + rows:] = pick(parity, one, two)
    a, b = shift_ref[0, 0], shift_ref[0, 1]
    span, step = 2 * rim, 32
    x_ref[:, :8] = jnp.zeros((2, 8, n), F32)
    x_ref[:, 8 + rows:] = jnp.zeros((2, 8, n), F32)
    for lo in (0, rows - span):
        for half in range(2):
            x_ref[half, 8 + lo:8 + lo + span] = dot(g_ref[half * rows + lo:half * rows + lo + span], ext_ref[...])
    for side, lo in ((0, 0), (1, rows - rim)):
        for k in range(0, rim, step):
            out = residual(x_ref, lo + k, step, rim, side == 1, side == 0, src_ref, sigma_ref, a, b)
            for half in range(2):
                r_ref[side, half, k:k + step] = out[half]
        blocks = [x_ref[half, 8 + lo:8 + lo + rim] for half in range(2)] + [r_ref[side, half] for half in range(2)]
        store_coded(msgs_ref.at[parity if side else 1 - parity], blocks)


def add_product(rows, g_ref, cols, er, ei, wr, wi, base, out_ref):
    block = rows // 3 if rows % 384 == 0 else rows
    for lo in range(0, rows, block):
        gr, gi = [jnp.concatenate([g_ref[half + lo:half + lo + block, c] for c in cols], axis=1) for half in (0, rows)]
        real = dot(gr, er) - dot(gi, ei)
        imag = dot(gr, ei) + dot(gi, er)
        out_ref[lo:lo + block] = base(lo, block) + (wr * real - wi * imag)


def middle_kernel(rim, shift_ref, weight_ref, g_ref, src_ref, ext_ref, outer_ref, sigma_ref, out_ref, x_ref, e_ref):
    rows, _ = src_ref.shape
    span, step = 2 * rim, 32
    a, b = shift_ref[0, 0], shift_ref[0, 1]
    wr, wi = 2.0 * weight_ref[0, 0], 2.0 * weight_ref[0, 1]
    if rows > 2 * span:
        for half in range(2):
            x_ref[half, 8 + span:8 + rows - span] = dot(g_ref[half * rows + span:(half + 1) * rows - span], ext_ref[...])
    for lo in range(rim, rows - rim, step):
        out = residual(x_ref, lo, step, rim, True, True, src_ref, sigma_ref, a, b)
        for half in range(2):
            e_ref[half, lo - rim:lo - rim + step] = out[half].astype(BF16)

    def base(lo, count):
        return wr * x_ref[0, 8 + lo:8 + lo + count] - wi * x_ref[1, 8 + lo:8 + lo + count]

    add_product(rows, g_ref, [slice(span, rows)], e_ref[0], e_ref[1], wr, wi, base, out_ref)


def last_kernel(rim, hops, weight_ref, g_ref, part_ref, x_ref, r_ref, got_ref, *rest):
    own_ref, msgs, u_ref, e_ref = rest[0], rest[1:1 + hops], rest[1 + hops], rest[2 + hops]
    rows, _ = part_ref.shape
    share = own_ref.shape[0]
    sub, pole = lax.axis_index("sub"), lax.axis_index("pole")
    parity = lax.rem(sub, 2)
    wr, wi = 2.0 * weight_ref[0, 0], 2.0 * weight_ref[0, 1]
    before_ref, after_ref = got_ref.at[1 - parity], got_ref.at[parity]
    inner_up = jnp.where(sub == 0, 0.0, 1.0)
    inner_down = jnp.where(sub == lax.axis_size("sub") - 1, 0.0, 1.0)
    up_scale = jnp.exp2(before_ref[4 * rim:4 * rim + 1] - TOP)
    down_scale = jnp.exp2(after_ref[4 * rim:4 * rim + 1] - TOP)
    at = lax.broadcasted_iota(jnp.int32, (rim, 1), 0)
    for half in range(2):
        x, r = slice(half * rim, (half + 1) * rim), slice((2 + half) * rim, (3 + half) * rim)
        xb, qb = before_ref[x] * up_scale, before_ref[r] * up_scale
        xa, qa = after_ref[x] * down_scale, after_ref[r] * down_scale
        low, high = x_ref[half, 8:8 + rim], x_ref[half, 8 + rows - rim:8 + rows]
        above = qb + low + jnp.where(at == rim - 1, low[:1], 0.0)
        below = qa + high + jnp.where(at == 0, high[rim - 1:], 0.0)
        head = r_ref[0, half] + xb + jnp.where(at == 0, xb[rim - 1:], 0.0)
        foot = r_ref[1, half] + xa + jnp.where(at == rim - 1, xa[:1], 0.0)
        e_ref[half, :rim] = (inner_up * above).astype(BF16)
        e_ref[half, rim:2 * rim] = head.astype(BF16)
        e_ref[half, 2 * rim:3 * rim] = foot.astype(BF16)
        e_ref[half, 3 * rim:] = (inner_down * below).astype(BF16)
    add_product(
        rows, g_ref, [slice(0, 2 * rim), slice(rows, rows + 2 * rim)], e_ref[0], e_ref[1], wr, wi,
        lambda lo, count: part_ref[lo:lo + count], u_ref,
    )
    own_ref[...] = u_ref[rows_of(pole, share)]
    for hop, ref in enumerate(msgs):
        store_coded(ref, [u_ref[rows_of(hop_target(pole, hop + 1, hops + 1), share)]])


def sum_kernel(own_ref, *rest):
    got, total_ref = rest[:-1], rest[-1]
    share = own_ref.shape[0]
    total = own_ref[...]
    for ref in got:
        if ref.shape[0] == share:
            total = total * ref[...]
        else:
            total = total + ref[:share] * jnp.exp2(ref[share:share + 1] - TOP)
    total_ref[...] = total.astype(total_ref.dtype)


def join_kernel(rim, own_ref, *rest):
    got, (src_ref, msg1_ref, msg2_ref) = rest[:-3], rest[-3:]
    share, rows, poles = own_ref.shape[0], src_ref.shape[0], len(got) + 1
    parity, pole = lax.rem(lax.axis_index("sub"), 2), lax.axis_index("pole")
    src_ref[rows_of(pole, share)] = own_ref[...]
    for hop, ref in enumerate(got):
        src_ref[rows_of(hop_source(pole, hop + 1, poles), share)] = ref[...]
    low, high = src_ref[:rim], src_ref[rows - rim:]
    msg1_ref[...] = pick(parity, high, low)
    msg2_ref[...] = pick(parity, low, high)


def shards(state, conductivity, pole_shift, pole_weight, order_list, inverse):
    rows, columns = state.shape
    order = order_list.shape[1]
    rim = (order - rows) // 2
    subs, poles = lax.axis_size("sub"), lax.axis_size("pole")
    share, hops = rows // poles, poles - 1
    n = columns // CHUNKS
    pairs1 = [(i ^ 1, i) for i in range(subs) if i ^ 1 < subs]
    pairs2 = [(j, i) for i in range(subs) for j in [((i + 1) ^ 1) - 1] if 0 <= j < subs]

    def exchange(one, two):
        one = lax.ppermute(one, "sub", pairs1)
        two = lax.ppermute(two, "sub", pairs2)
        return one, two

    one, two, sigma, sigma_share, order_row, *sources = call(
        functools.partial(start_kernel, rim),
        [((rim, columns), BF16), ((rim, columns), BF16), ((rows, n), F32), ((share, n), F32), ((1, order), F32)]
        + [((rows, n), F32)] * CHUNKS,
        [(VMEM, conductivity), (VMEM, order_list), (VMEM, state)], moved=8 * rows * columns,
    )
    first_halo = exchange(one, two)
    (g,) = call(
        setup_kernel, [((2 * rows, order), BF16)], [(VMEM, order_row), (VMEM, inverse)],
        flops=4 * rows * order * order, moved=6 * rows * order,
    )

    def sweep(source, got, lane):
        ext, x, r, msgs = call(
            functools.partial(edge_kernel, rim, lane),
            [((order, n), BF16), ((2, rows + 16, n), F32), ((2, 2, rim, n), F32), ((2, 4 * rim + TAIL, n), F32)],
            [(SMEM, pole_shift), (VMEM, g), (VMEM, source), (VMEM, got[0]), (VMEM, got[1]), (VMEM, sigma)],
            flops=16 * rim * order * n, moved=4 * rows * order,
        )
        got = exchange(msgs[0].astype(F16), msgs[1].astype(F16))
        part, x = call(
            functools.partial(middle_kernel, rim), [((rows, n), F32), ((2, rows + 16, n), F32)],
            [(SMEM, pole_shift), (SMEM, pole_weight), (VMEM, g), (VMEM, source), (VMEM, ext), (VMEM, x), (VMEM, sigma)],
            [pltpu.VMEM((2, rows - 2 * rim, n), BF16)],
            flops=8 * rows * rows * n, moved=4 * rows * order, alias={5: 1},
        )
        return call(
            functools.partial(last_kernel, rim, hops),
            [((share, n), F32)] + [((share + TAIL, n), F32)] * hops,
            [(SMEM, pole_weight), (VMEM, g), (VMEM, part), (VMEM, x), (VMEM, r), (VMEM, jnp.stack(got).astype(F32))],
            [pltpu.VMEM((rows, n), F32), pltpu.VMEM((2, 4 * rim, n), BF16)],
            flops=8 * rows * 4 * rim * n, moved=4 * rows * order,
        )

    def reduced(sent, factor):
        own, *sent = sent
        got = []
        for hop, block in enumerate(sent):
            got.append(lax.ppermute(block.astype(F16), "pole", hop_pairs(hop + 1, poles)))
        ins = [own] + [x.astype(F32) for x in got] + factor
        return call(
            sum_kernel, [((share, n), BF16 if factor else F32)], [(VMEM, x) for x in ins],
            moved=4 * rows * n,
        )[0]

    def gathered(own):
        got = []
        for hop in range(hops):
            got.append(lax.ppermute(own, "pole", hop_pairs(hop + 1, poles)))
        return call(
            functools.partial(join_kernel, rim),
            [((rows, n), BF16), ((rim, n), BF16), ((rim, n), BF16)],
            [(VMEM, own)] + [(VMEM, x) for x in got], moved=4 * rows * n,
        )

    results = []
    for chunk in range(CHUNKS):
        source, halo = sources[chunk], first_halo
        for step in range(STEPS):
            factor = [sigma_share] if step + 1 < STEPS else []
            total = reduced(sweep(source, halo, 0 if step else chunk * n), factor)
            if step + 1 < STEPS:
                source, one, two = gathered(total)
                halo = exchange(one, two)
        results.append(total)
    return jnp.concatenate(results, axis=1) if CHUNKS > 1 else results[0]


def solution(mesh):
    placed = (
        P("sub", None),
        P("sub"),
        P("pole", None),
        P("pole", None),
        P("sub", None),
        P("pole", "sub", None),
    )
    return jax.shard_map(
        shards, mesh=mesh, in_specs=placed, out_specs=P(("sub", "pole"), None), check_vma=False
    )
```

```python
import functools

import jax
import jax.numpy as jnp
from jax import lax
from jax.experimental import pallas as pl
from jax.experimental.pallas import tpu as pltpu
from jax.sharding import PartitionSpec as P


STEPS = 2
PARTS = (1, 1)
TAIL = 8
TOP = 12.0
BF16 = jnp.bfloat16
F16 = jnp.float16
F32 = jnp.float32
VMEM = pl.BlockSpec(memory_space=pltpu.VMEM)
SMEM = pl.BlockSpec(memory_space=pltpu.SMEM)


def split_at(chunk):
    return chunk == 0


def call(kernel, outs, ins, scratch=(), flops=0, moved=0, alias=()):
    return pl.pallas_call(
        kernel,
        out_shape=[jax.ShapeDtypeStruct(s, d) for s, d in outs],
        in_specs=[s for s, _ in ins],
        out_specs=[VMEM] * len(outs),
        scratch_shapes=list(scratch),
        input_output_aliases=dict(alias),
        compiler_params=pltpu.CompilerParams(vmem_limit_bytes=16 * 2**20),
        cost_estimate=pl.CostEstimate(flops=flops, bytes_accessed=moved, transcendentals=0),
    )(*[a for _, a in ins])


def dot(a, b):
    return jnp.dot(a, b, preferred_element_type=F32)


def store_coded(ref, blocks):
    top = functools.reduce(jnp.maximum, [jnp.max(jnp.abs(b), axis=0, keepdims=True) for b in blocks])
    power = jnp.ceil(jnp.log2(jnp.maximum(top, 1e-30)))
    scale, at = jnp.exp2(TOP - power), 0
    for block in blocks:
        ref[at:at + block.shape[0]] = block * scale
        at += block.shape[0]
    ref[at:] = jnp.broadcast_to(power, (TAIL, top.shape[1]))


def pick(flag, a, b):
    return jnp.where(flag == 0, a, b)


def hop_target(pole, hop, poles):
    return pole ^ hop if poles & (poles - 1) == 0 else lax.rem(pole + hop, poles)


def hop_source(pole, hop, poles):
    return pole ^ hop if poles & (poles - 1) == 0 else lax.rem(pole + poles - hop, poles)


def hop_pairs(hop, poles):
    return [(i, i ^ hop if poles & (poles - 1) == 0 else (i + hop) % poles) for i in range(poles)]


def rows_of(index, share):
    return pl.ds(pl.multiple_of(index * share, share), share)


def column(row, count):
    return jnp.transpose(jnp.broadcast_to(row, (8, count)))[:, :1]


def start_kernel(rim, sigma_ref, order_ref, state_ref, msg1_ref, msg2_ref, wide_ref, share_ref, row_ref, *chunks):
    rows, share, lane = state_ref.shape[0], share_ref.shape[0], 0
    parity = lax.rem(lax.axis_index("sub"), 2)
    sigma = column(sigma_ref[...].reshape(1, rows), rows)
    low = (state_ref[:rim] * sigma[:rim]).astype(BF16)
    high = (state_ref[rows - rim:] * sigma[rows - rim:]).astype(BF16)
    msg1_ref[...] = pick(parity, high, low)
    msg2_ref[...] = pick(parity, low, high)
    wide_ref[...] = jnp.broadcast_to(sigma, wide_ref.shape)
    share_ref[...] = wide_ref[rows_of(lax.axis_index("pole"), share)]
    row_ref[...] = order_ref[...].astype(F32)
    for ref in chunks:
        ref[...] = state_ref[:, lane:lane + ref.shape[1]] * sigma
        lane += ref.shape[1]


def setup_kernel(row_ref, inv_ref, g_ref):
    rows, width = inv_ref.shape[1], inv_ref.shape[2] // 2
    ids = lax.broadcasted_iota(jnp.int32, (width, width), 1)
    place = (column(row_ref[...], width).astype(jnp.int32) == ids).astype(BF16)
    g_ref[:rows] = dot(inv_ref[0, :, :width], place).astype(BF16)
    g_ref[rows:] = dot(inv_ref[0, :, width:], place).astype(BF16)


def stencil(x_ref, half, lo, count, rim, far_up, far_down):
    def row(shift):
        return x_ref[half, 8 + lo + shift:8 + lo + shift + count]

    mid = 4.0 * row(0) - row(-1) - row(1)
    if far_up:
        mid = mid - row(-rim)
    if far_down:
        mid = mid - row(rim)
    return mid


def residual(x_ref, lo, count, rim, far_up, far_down, src_ref, sigma_ref, a, b):
    at = slice(lo, lo + count)
    xr, xi = x_ref[0, 8 + lo:8 + lo + count], x_ref[1, 8 + lo:8 + lo + count]
    sigma = sigma_ref[at, :src_ref.shape[1]]
    real = src_ref[at].astype(F32) - stencil(x_ref, 0, lo, count, rim, far_up, far_down) - sigma * (a * xr - b * xi)
    imag = -stencil(x_ref, 1, lo, count, rim, far_up, far_down) - sigma * (b * xr + a * xi)
    return real, imag


def edge_kernel(rim, lane, shift_ref, g_ref, src_ref, one_ref, two_ref, sigma_ref, ext_ref, x_ref, r_ref, msgs_ref):
    rows, n = src_ref.shape
    parity = lax.rem(lax.axis_index("sub"), 2)
    one, two = one_ref[:, lane:lane + n], two_ref[:, lane:lane + n]
    ext_ref[:rim] = pick(parity, two, one)
    ext_ref[rim:rim + rows] = src_ref[...].astype(BF16)
    ext_ref[rim + rows:] = pick(parity, one, two)
    a, b = shift_ref[0, 0], shift_ref[0, 1]
    span, step = 2 * rim, 32
    x_ref[:, :8] = jnp.zeros((2, 8, n), F32)
    x_ref[:, 8 + rows:] = jnp.zeros((2, 8, n), F32)
    for lo in (0, rows - span):
        for half in range(2):
            x_ref[half, 8 + lo:8 + lo + span] = dot(g_ref[half * rows + lo:half * rows + lo + span], ext_ref[...])
    for side, lo in ((0, 0), (1, rows - rim)):
        for k in range(0, rim, step):
            out = residual(x_ref, lo + k, step, rim, side == 1, side == 0, src_ref, sigma_ref, a, b)
            for half in range(2):
                r_ref[side, half, k:k + step] = out[half]
        blocks = [x_ref[half, 8 + lo:8 + lo + rim] for half in range(2)] + [r_ref[side, half] for half in range(2)]
        store_coded(msgs_ref.at[parity if side else 1 - parity], blocks)


def add_product(rows, g_ref, cols, er, ei, wr, wi, base, out_ref):
    block = rows // 3 if rows % 384 == 0 else rows
    for lo in range(0, rows, block):
        gr, gi = [jnp.concatenate([g_ref[half + lo:half + lo + block, c] for c in cols], axis=1) for half in (0, rows)]
        real = dot(gr, er) - dot(gi, ei)
        imag = dot(gr, ei) + dot(gi, er)
        out_ref[lo:lo + block] = base(lo, block) + (wr * real - wi * imag)


def inner_residual(rim, shift_ref, g_ref, src_ref, ext_ref, sigma_ref, x_ref, e_ref, at):
    rows = src_ref.shape[0]
    span, step = 2 * rim, 32
    a, b = shift_ref[0, 0], shift_ref[0, 1]
    if rows > 2 * span:
        for half in range(2):
            x_ref[half, 8 + span:8 + rows - span] = dot(g_ref[half * rows + span:(half + 1) * rows - span], ext_ref[...])
    for lo in range(rim, rows - rim, step):
        out = residual(x_ref, lo, step, rim, True, True, src_ref, sigma_ref, a, b)
        for half in range(2):
            e_ref[half, at + lo - rim:at + lo - rim + step] = out[half].astype(BF16)


def outer_residual(rim, x_ref, r_ref, got_ref, e_ref, after_at):
    rows = x_ref.shape[1] - 16
    sub = lax.axis_index("sub")
    parity = lax.rem(sub, 2)
    before_ref, after_ref = got_ref.at[1 - parity], got_ref.at[parity]
    inner_up = jnp.where(sub == 0, 0.0, 1.0)
    inner_down = jnp.where(sub == lax.axis_size("sub") - 1, 0.0, 1.0)
    up_scale = jnp.exp2(before_ref[4 * rim:4 * rim + 1] - TOP)
    down_scale = jnp.exp2(after_ref[4 * rim:4 * rim + 1] - TOP)
    at = lax.broadcasted_iota(jnp.int32, (rim, 1), 0)
    for half in range(2):
        x, r = slice(half * rim, (half + 1) * rim), slice((2 + half) * rim, (3 + half) * rim)
        xb, qb = before_ref[x] * up_scale, before_ref[r] * up_scale
        xa, qa = after_ref[x] * down_scale, after_ref[r] * down_scale
        low, high = x_ref[half, 8:8 + rim], x_ref[half, 8 + rows - rim:8 + rows]
        above = qb + low + jnp.where(at == rim - 1, low[:1], 0.0)
        below = qa + high + jnp.where(at == 0, high[rim - 1:], 0.0)
        head = r_ref[0, half] + xb + jnp.where(at == 0, xb[rim - 1:], 0.0)
        foot = r_ref[1, half] + xa + jnp.where(at == rim - 1, xa[:1], 0.0)
        e_ref[half, :rim] = (inner_up * above).astype(BF16)
        e_ref[half, rim:2 * rim] = head.astype(BF16)
        e_ref[half, after_at:after_at + rim] = foot.astype(BF16)
        e_ref[half, after_at + rim:after_at + 2 * rim] = (inner_down * below).astype(BF16)


def store_shares(u_ref, own_ref, msgs):
    share, poles, pole = own_ref.shape[0], len(msgs) + 1, lax.axis_index("pole")
    own_ref[...] = u_ref[rows_of(pole, share)]
    for hop, ref in enumerate(msgs):
        store_coded(ref, [u_ref[rows_of(hop_target(pole, hop + 1, poles), share)]])


def middle_kernel(rim, shift_ref, weight_ref, g_ref, src_ref, ext_ref, outer_ref, sigma_ref, out_ref, x_ref, e_ref):
    rows, _ = src_ref.shape
    wr, wi = 2.0 * weight_ref[0, 0], 2.0 * weight_ref[0, 1]
    inner_residual(rim, shift_ref, g_ref, src_ref, ext_ref, sigma_ref, x_ref, e_ref, 0)

    def base(lo, count):
        return wr * x_ref[0, 8 + lo:8 + lo + count] - wi * x_ref[1, 8 + lo:8 + lo + count]

    add_product(rows, g_ref, [slice(2 * rim, rows)], e_ref[0], e_ref[1], wr, wi, base, out_ref)


def last_kernel(rim, hops, weight_ref, g_ref, part_ref, x_ref, r_ref, got_ref, *rest):
    own_ref, msgs, u_ref, e_ref = rest[0], rest[1:1 + hops], rest[1 + hops], rest[2 + hops]
    rows, _ = part_ref.shape
    wr, wi = 2.0 * weight_ref[0, 0], 2.0 * weight_ref[0, 1]
    outer_residual(rim, x_ref, r_ref, got_ref, e_ref, rim * 2)
    add_product(
        rows, g_ref, [slice(0, 2 * rim), slice(rows, rows + 2 * rim)], e_ref[0], e_ref[1], wr, wi,
        lambda lo, count: part_ref[lo:lo + count], u_ref,
    )
    store_shares(u_ref, own_ref, msgs)


def tail_kernel(rim, hops, shift_ref, weight_ref, g_ref, src_ref, ext_ref, outer_ref, sigma_ref, r_ref, got_ref, *rest):
    own_ref, msgs, x_ref, u_ref, e_ref = rest[0], rest[1:1 + hops], rest[1 + hops], rest[2 + hops], rest[3 + hops]
    rows, _ = src_ref.shape
    span = 2 * rim
    wr, wi = 2.0 * weight_ref[0, 0], 2.0 * weight_ref[0, 1]
    inner_residual(rim, shift_ref, g_ref, src_ref, ext_ref, sigma_ref, x_ref, e_ref, span)
    outer_residual(rim, x_ref, r_ref, got_ref, e_ref, rows)

    def base(lo, count):
        return wr * x_ref[0, 8 + lo:8 + lo + count] - wi * x_ref[1, 8 + lo:8 + lo + count]

    add_product(rows, g_ref, [slice(0, rows + span)], e_ref[0], e_ref[1], wr, wi, base, u_ref)
    store_shares(u_ref, own_ref, msgs)


def summed(own_ref, got):
    share = own_ref.shape[0]
    total = own_ref[...]
    for ref in got:
        total = total + ref[:share] * jnp.exp2(ref[share:share + 1] - TOP)
    return total


def sum_kernel(factor_ref, own_ref, *rest):
    got, total_ref = rest[:-1], rest[-1]
    total_ref[...] = (summed(own_ref, got) * factor_ref[:, :total_ref.shape[1]]).astype(BF16)


def final_kernel(*refs):
    sets, out_ref, lane = refs[:-1], refs[-1], 0
    each = len(sets) // len(PARTS)
    for at in range(0, len(sets), each):
        n = sets[at].shape[1]
        out_ref[:, lane:lane + n] = summed(sets[at], sets[at + 1:at + each])
        lane += n


def join_kernel(rim, own_ref, *rest):
    got, (src_ref, msg1_ref, msg2_ref) = rest[:-3], rest[-3:]
    share, rows, poles = own_ref.shape[0], src_ref.shape[0], len(got) + 1
    parity, pole = lax.rem(lax.axis_index("sub"), 2), lax.axis_index("pole")
    src_ref[rows_of(pole, share)] = own_ref[...]
    for hop, ref in enumerate(got):
        src_ref[rows_of(hop_source(pole, hop + 1, poles), share)] = ref[...]
    low, high = src_ref[:rim], src_ref[rows - rim:]
    msg1_ref[...] = pick(parity, high, low)
    msg2_ref[...] = pick(parity, low, high)


def shards(state, conductivity, pole_shift, pole_weight, order_list, inverse):
    rows, columns = state.shape
    order = order_list.shape[1]
    rim = (order - rows) // 2
    subs, poles = lax.axis_size("sub"), lax.axis_size("pole")
    share, hops = rows // poles, poles - 1
    widths = [columns * part // sum(PARTS) for part in PARTS]
    widest = max(widths)
    pairs1 = [(i ^ 1, i) for i in range(subs) if i ^ 1 < subs]
    pairs2 = [(j, i) for i in range(subs) for j in [((i + 1) ^ 1) - 1] if 0 <= j < subs]

    def exchange(one, two):
        one = lax.ppermute(one, "sub", pairs1)
        two = lax.ppermute(two, "sub", pairs2)
        return one, two

    one, two, sigma, sigma_share, order_row, *sources = call(
        functools.partial(start_kernel, rim),
        [((rim, columns), BF16), ((rim, columns), BF16), ((rows, widest), F32), ((share, widest), F32), ((1, order), F32)]
        + [((rows, n), F32) for n in widths],
        [(VMEM, conductivity), (VMEM, order_list), (VMEM, state)], moved=8 * rows * columns,
    )
    first_halo = exchange(one, two)
    (g,) = call(
        setup_kernel, [((2 * rows, order), BF16)], [(VMEM, order_row), (VMEM, inverse)],
        flops=4 * rows * order * order, moved=6 * rows * order,
    )

    def sweep(source, got, lane, split):
        n = source.shape[1]
        ext, x, r, msgs = call(
            functools.partial(edge_kernel, rim, lane),
            [((order, n), BF16), ((2, rows + 16, n), F32), ((2, 2, rim, n), F32), ((2, 4 * rim + TAIL, n), F32)],
            [(SMEM, pole_shift), (VMEM, g), (VMEM, source), (VMEM, got[0]), (VMEM, got[1]), (VMEM, sigma)],
            flops=16 * rim * order * n, moved=4 * rows * order,
        )
        got = exchange(msgs[0].astype(F16), msgs[1].astype(F16))
        shares = [((share, n), F32)] + [((share + TAIL, n), F32)] * hops
        if not split:
            return call(
                functools.partial(tail_kernel, rim, hops), shares + [((2, rows + 16, n), F32)],
                [(SMEM, pole_shift), (SMEM, pole_weight), (VMEM, g), (VMEM, source), (VMEM, ext), (VMEM, x),
                 (VMEM, sigma), (VMEM, r), (VMEM, jnp.stack(got).astype(F32))],
                [pltpu.VMEM((rows, n), F32), pltpu.VMEM((2, order, n), BF16)],
                flops=8 * rows * order * n, moved=4 * rows * order, alias={5: 1 + hops},
            )[:-1]
        part, x = call(
            functools.partial(middle_kernel, rim), [((rows, n), F32), ((2, rows + 16, n), F32)],
            [(SMEM, pole_shift), (SMEM, pole_weight), (VMEM, g), (VMEM, source), (VMEM, ext), (VMEM, x), (VMEM, sigma)],
            [pltpu.VMEM((2, rows - 2 * rim, n), BF16)],
            flops=8 * rows * rows * n, moved=4 * rows * order, alias={5: 1},
        )
        return call(
            functools.partial(last_kernel, rim, hops), shares,
            [(SMEM, pole_weight), (VMEM, g), (VMEM, part), (VMEM, x), (VMEM, r), (VMEM, jnp.stack(got).astype(F32))],
            [pltpu.VMEM((rows, n), F32), pltpu.VMEM((2, 4 * rim, n), BF16)],
            flops=8 * rows * 4 * rim * n, moved=4 * rows * order,
        )

    def moved(sent):
        own, *sent = sent
        got = []
        for hop, block in enumerate(sent):
            got.append(lax.ppermute(block.astype(F16), "pole", hop_pairs(hop + 1, poles)))
        return [own] + [x.astype(F32) for x in got]

    def gathered(own):
        got, n = [], own.shape[1]
        for hop in range(hops):
            got.append(lax.ppermute(own, "pole", hop_pairs(hop + 1, poles)))
        return call(
            functools.partial(join_kernel, rim),
            [((rows, n), BF16), ((rim, n), BF16), ((rim, n), BF16)],
            [(VMEM, own)] + [(VMEM, x) for x in got], moved=4 * rows * n,
        )

    results, lane = [], 0
    for chunk, n in enumerate(widths):
        source, halo = sources[chunk], first_halo
        for step in range(STEPS):
            terms = moved(sweep(source, halo, 0 if step else lane, split_at(chunk)))
            if step + 1 < STEPS:
                (total,) = call(
                    sum_kernel, [((share, n), BF16)], [(VMEM, x) for x in [sigma_share] + terms],
                    moved=4 * rows * n,
                )
                source, one, two = gathered(total)
                halo = exchange(one, two)
        results.extend(terms)
        lane += n
    return call(final_kernel, [((share, columns), F32)], [(VMEM, x) for x in results], moved=4 * rows * columns)[0]


def solution(mesh):
    placed = (
        P("sub", None),
        P("sub"),
        P("pole", None),
        P("pole", None),
        P("sub", None),
        P("pole", "sub", None),
    )
    return jax.shard_map(
        shards, mesh=mesh, in_specs=placed, out_specs=P(("sub", "pole"), None), check_vma=False
    )
```

```python
import functools

import jax
import jax.numpy as jnp
from jax import lax
from jax.experimental import pallas as pl
from jax.experimental.pallas import tpu as pltpu
from jax.sharding import PartitionSpec as P


STEPS = 2
PARTS = (1, 1)
TAIL = 8
TOP = 12.0
BF16 = jnp.bfloat16
F16 = jnp.float16
F32 = jnp.float32
VMEM = pl.BlockSpec(memory_space=pltpu.VMEM)
SMEM = pl.BlockSpec(memory_space=pltpu.SMEM)


def split_at(chunk, step):
    return chunk == 0 or step == 0


def call(kernel, outs, ins, scratch=(), flops=0, moved=0, alias=()):
    return pl.pallas_call(
        kernel,
        out_shape=[jax.ShapeDtypeStruct(s, d) for s, d in outs],
        in_specs=[s for s, _ in ins],
        out_specs=[VMEM] * len(outs),
        scratch_shapes=list(scratch),
        input_output_aliases=dict(alias),
        compiler_params=pltpu.CompilerParams(vmem_limit_bytes=16 * 2**20),
        cost_estimate=pl.CostEstimate(flops=flops, bytes_accessed=moved, transcendentals=0),
    )(*[a for _, a in ins])


def dot(a, b):
    return jnp.dot(a, b, preferred_element_type=F32)


def store_coded(ref, blocks):
    top = functools.reduce(jnp.maximum, [jnp.max(jnp.abs(b), axis=0, keepdims=True) for b in blocks])
    power = jnp.ceil(jnp.log2(jnp.maximum(top, 1e-30)))
    scale, at = jnp.exp2(TOP - power), 0
    for block in blocks:
        ref[at:at + block.shape[0]] = block * scale
        at += block.shape[0]
    ref[at:] = jnp.broadcast_to(power, (TAIL, top.shape[1]))


def pick(flag, a, b):
    return jnp.where(flag == 0, a, b)


def hop_target(pole, hop, poles):
    return pole ^ hop if poles & (poles - 1) == 0 else lax.rem(pole + hop, poles)


def hop_source(pole, hop, poles):
    return pole ^ hop if poles & (poles - 1) == 0 else lax.rem(pole + poles - hop, poles)


def hop_pairs(hop, poles):
    return [(i, i ^ hop if poles & (poles - 1) == 0 else (i + hop) % poles) for i in range(poles)]


def rows_of(index, share):
    return pl.ds(pl.multiple_of(index * share, share), share)


def column(row, count):
    return jnp.transpose(jnp.broadcast_to(row, (8, count)))[:, :1]


def start_kernel(rim, sigma_ref, order_ref, state_ref, msg1_ref, msg2_ref, wide_ref, share_ref, row_ref, *chunks):
    rows, share, lane = state_ref.shape[0], share_ref.shape[0], 0
    parity = lax.rem(lax.axis_index("sub"), 2)
    sigma = column(sigma_ref[...].reshape(1, rows), rows)
    low = (state_ref[:rim] * sigma[:rim]).astype(BF16)
    high = (state_ref[rows - rim:] * sigma[rows - rim:]).astype(BF16)
    msg1_ref[...] = pick(parity, high, low)
    msg2_ref[...] = pick(parity, low, high)
    wide_ref[...] = jnp.broadcast_to(sigma, wide_ref.shape)
    share_ref[...] = wide_ref[rows_of(lax.axis_index("pole"), share)]
    row_ref[...] = order_ref[...].astype(F32)
    for ref in chunks:
        ref[...] = state_ref[:, lane:lane + ref.shape[1]] * sigma
        lane += ref.shape[1]


def places(row_ref):
    width = row_ref.shape[1]
    ids = lax.broadcasted_iota(jnp.int32, (width, width), 1)
    return (column(row_ref[...], width).astype(jnp.int32) == ids).astype(BF16)


def setup_kernel(row_ref, inv_ref, outer_ref):
    rows, width = inv_ref.shape[1], row_ref.shape[1]
    span, place = outer_ref.shape[0] // 4, places(row_ref)
    for half in range(2):
        part = inv_ref.at[0, :, half * width:(half + 1) * width]
        for side, lo in ((0, 0), (1, rows - span)):
            at = (2 * half + side) * span
            outer_ref[at:at + span] = dot(part[lo:lo + span], place).astype(BF16)


def inner_kernel(row_ref, inv_ref, outer_ref, g_ref):
    rows, width = inv_ref.shape[1], row_ref.shape[1]
    span, place = outer_ref.shape[0] // 4, places(row_ref)
    for half in range(2):
        part = inv_ref.at[0, :, half * width:(half + 1) * width]
        for side, lo in ((0, 0), (1, rows - span)):
            at = (2 * half + side) * span
            g_ref[half * rows + lo:half * rows + lo + span] = outer_ref[at:at + span]
        if rows > 2 * span:
            g_ref[half * rows + span:(half + 1) * rows - span] = dot(part[span:rows - span], place).astype(BF16)


def stencil(x_ref, half, lo, count, rim, far_up, far_down):
    def row(shift):
        return x_ref[half, 8 + lo + shift:8 + lo + shift + count]

    mid = 4.0 * row(0) - row(-1) - row(1)
    if far_up:
        mid = mid - row(-rim)
    if far_down:
        mid = mid - row(rim)
    return mid


def residual(x_ref, lo, count, rim, far_up, far_down, src_ref, sigma_ref, a, b):
    at = slice(lo, lo + count)
    xr, xi = x_ref[0, 8 + lo:8 + lo + count], x_ref[1, 8 + lo:8 + lo + count]
    sigma = sigma_ref[at, :src_ref.shape[1]]
    real = src_ref[at].astype(F32) - stencil(x_ref, 0, lo, count, rim, far_up, far_down) - sigma * (a * xr - b * xi)
    imag = -stencil(x_ref, 1, lo, count, rim, far_up, far_down) - sigma * (b * xr + a * xi)
    return real, imag


def edge_kernel(rim, lane, shift_ref, g_ref, src_ref, one_ref, two_ref, sigma_ref, ext_ref, x_ref, r_ref, msgs_ref):
    rows, n = src_ref.shape
    parity = lax.rem(lax.axis_index("sub"), 2)
    one, two = one_ref[:, lane:lane + n], two_ref[:, lane:lane + n]
    ext_ref[:rim] = pick(parity, two, one)
    ext_ref[rim:rim + rows] = src_ref[...].astype(BF16)
    ext_ref[rim + rows:] = pick(parity, one, two)
    a, b = shift_ref[0, 0], shift_ref[0, 1]
    span, step = 2 * rim, 32
    x_ref[:, :8] = jnp.zeros((2, 8, n), F32)
    x_ref[:, 8 + rows:] = jnp.zeros((2, 8, n), F32)
    for lo in (0, rows - span):
        for half in range(2):
            at = half * rows + lo if g_ref.shape[0] == 2 * rows else (2 * half + (lo > 0)) * span
            x_ref[half, 8 + lo:8 + lo + span] = dot(g_ref[at:at + span], ext_ref[...])
    for side, lo in ((0, 0), (1, rows - rim)):
        for k in range(0, rim, step):
            out = residual(x_ref, lo + k, step, rim, side == 1, side == 0, src_ref, sigma_ref, a, b)
            for half in range(2):
                r_ref[side, half, k:k + step] = out[half]
        blocks = [x_ref[half, 8 + lo:8 + lo + rim] for half in range(2)] + [r_ref[side, half] for half in range(2)]
        store_coded(msgs_ref.at[parity if side else 1 - parity], blocks)


def add_product(rows, g_ref, cols, er, ei, wr, wi, base, out_ref):
    block = rows // 3 if rows % 384 == 0 else rows
    for lo in range(0, rows, block):
        gr, gi = [jnp.concatenate([g_ref[half + lo:half + lo + block, c] for c in cols], axis=1) for half in (0, rows)]
        real = dot(gr, er) - dot(gi, ei)
        imag = dot(gr, ei) + dot(gi, er)
        out_ref[lo:lo + block] = base(lo, block) + (wr * real - wi * imag)


def inner_residual(rim, shift_ref, g_ref, src_ref, ext_ref, sigma_ref, x_ref, e_ref, at):
    rows = src_ref.shape[0]
    span, step = 2 * rim, 32
    a, b = shift_ref[0, 0], shift_ref[0, 1]
    if rows > 2 * span:
        for half in range(2):
            x_ref[half, 8 + span:8 + rows - span] = dot(g_ref[half * rows + span:(half + 1) * rows - span], ext_ref[...])
    for lo in range(rim, rows - rim, step):
        out = residual(x_ref, lo, step, rim, True, True, src_ref, sigma_ref, a, b)
        for half in range(2):
            e_ref[half, at + lo - rim:at + lo - rim + step] = out[half].astype(BF16)


def outer_residual(rim, x_ref, r_ref, got_ref, e_ref, after_at):
    rows = x_ref.shape[1] - 16
    sub = lax.axis_index("sub")
    parity = lax.rem(sub, 2)
    before_ref, after_ref = got_ref.at[1 - parity], got_ref.at[parity]
    inner_up = jnp.where(sub == 0, 0.0, 1.0)
    inner_down = jnp.where(sub == lax.axis_size("sub") - 1, 0.0, 1.0)
    up_scale = jnp.exp2(before_ref[4 * rim:4 * rim + 1] - TOP)
    down_scale = jnp.exp2(after_ref[4 * rim:4 * rim + 1] - TOP)
    at = lax.broadcasted_iota(jnp.int32, (rim, 1), 0)
    for half in range(2):
        x, r = slice(half * rim, (half + 1) * rim), slice((2 + half) * rim, (3 + half) * rim)
        xb, qb = before_ref[x] * up_scale, before_ref[r] * up_scale
        xa, qa = after_ref[x] * down_scale, after_ref[r] * down_scale
        low, high = x_ref[half, 8:8 + rim], x_ref[half, 8 + rows - rim:8 + rows]
        above = qb + low + jnp.where(at == rim - 1, low[:1], 0.0)
        below = qa + high + jnp.where(at == 0, high[rim - 1:], 0.0)
        head = r_ref[0, half] + xb + jnp.where(at == 0, xb[rim - 1:], 0.0)
        foot = r_ref[1, half] + xa + jnp.where(at == rim - 1, xa[:1], 0.0)
        e_ref[half, :rim] = (inner_up * above).astype(BF16)
        e_ref[half, rim:2 * rim] = head.astype(BF16)
        e_ref[half, after_at:after_at + rim] = foot.astype(BF16)
        e_ref[half, after_at + rim:after_at + 2 * rim] = (inner_down * below).astype(BF16)


def store_shares(u_ref, own_ref, msgs):
    share, poles, pole = own_ref.shape[0], len(msgs) + 1, lax.axis_index("pole")
    own_ref[...] = u_ref[rows_of(pole, share)]
    for hop, ref in enumerate(msgs):
        store_coded(ref, [u_ref[rows_of(hop_target(pole, hop + 1, poles), share)]])


def middle_kernel(rim, shift_ref, weight_ref, g_ref, src_ref, ext_ref, outer_ref, sigma_ref, out_ref, x_ref, e_ref):
    rows, _ = src_ref.shape
    wr, wi = 2.0 * weight_ref[0, 0], 2.0 * weight_ref[0, 1]
    inner_residual(rim, shift_ref, g_ref, src_ref, ext_ref, sigma_ref, x_ref, e_ref, 0)

    def base(lo, count):
        return wr * x_ref[0, 8 + lo:8 + lo + count] - wi * x_ref[1, 8 + lo:8 + lo + count]

    add_product(rows, g_ref, [slice(2 * rim, rows)], e_ref[0], e_ref[1], wr, wi, base, out_ref)


def last_kernel(rim, hops, weight_ref, g_ref, part_ref, x_ref, r_ref, got_ref, *rest):
    own_ref, msgs, u_ref, e_ref = rest[0], rest[1:1 + hops], rest[1 + hops], rest[2 + hops]
    rows, _ = part_ref.shape
    wr, wi = 2.0 * weight_ref[0, 0], 2.0 * weight_ref[0, 1]
    outer_residual(rim, x_ref, r_ref, got_ref, e_ref, rim * 2)
    add_product(
        rows, g_ref, [slice(0, 2 * rim), slice(rows, rows + 2 * rim)], e_ref[0], e_ref[1], wr, wi,
        lambda lo, count: part_ref[lo:lo + count], u_ref,
    )
    store_shares(u_ref, own_ref, msgs)


def tail_kernel(rim, hops, shift_ref, weight_ref, g_ref, src_ref, ext_ref, outer_ref, sigma_ref, r_ref, got_ref, *rest):
    own_ref, msgs, x_ref, u_ref, e_ref = rest[0], rest[1:1 + hops], rest[1 + hops], rest[2 + hops], rest[3 + hops]
    rows, _ = src_ref.shape
    span = 2 * rim
    wr, wi = 2.0 * weight_ref[0, 0], 2.0 * weight_ref[0, 1]
    inner_residual(rim, shift_ref, g_ref, src_ref, ext_ref, sigma_ref, x_ref, e_ref, span)
    outer_residual(rim, x_ref, r_ref, got_ref, e_ref, rows)

    def base(lo, count):
        return wr * x_ref[0, 8 + lo:8 + lo + count] - wi * x_ref[1, 8 + lo:8 + lo + count]

    add_product(rows, g_ref, [slice(0, rows + span)], e_ref[0], e_ref[1], wr, wi, base, u_ref)
    store_shares(u_ref, own_ref, msgs)


def summed(own_ref, got):
    share = own_ref.shape[0]
    total = own_ref[...]
    for ref in got:
        total = total + ref[:share] * jnp.exp2(ref[share:share + 1] - TOP)
    return total


def sum_kernel(factor_ref, own_ref, *rest):
    got, total_ref = rest[:-1], rest[-1]
    total_ref[...] = (summed(own_ref, got) * factor_ref[:, :total_ref.shape[1]]).astype(BF16)


def final_kernel(*refs):
    sets, out_ref, lane = refs[:-1], refs[-1], 0
    each = len(sets) // len(PARTS)
    for at in range(0, len(sets), each):
        n = sets[at].shape[1]
        out_ref[:, lane:lane + n] = summed(sets[at], sets[at + 1:at + each])
        lane += n


def join_kernel(rim, own_ref, *rest):
    got, (src_ref, msg1_ref, msg2_ref) = rest[:-3], rest[-3:]
    share, rows, poles = own_ref.shape[0], src_ref.shape[0], len(got) + 1
    parity, pole = lax.rem(lax.axis_index("sub"), 2), lax.axis_index("pole")
    src_ref[rows_of(pole, share)] = own_ref[...]
    for hop, ref in enumerate(got):
        src_ref[rows_of(hop_source(pole, hop + 1, poles), share)] = ref[...]
    low, high = src_ref[:rim], src_ref[rows - rim:]
    msg1_ref[...] = pick(parity, high, low)
    msg2_ref[...] = pick(parity, low, high)


def shards(state, conductivity, pole_shift, pole_weight, order_list, inverse):
    rows, columns = state.shape
    order = order_list.shape[1]
    rim = (order - rows) // 2
    subs, poles = lax.axis_size("sub"), lax.axis_size("pole")
    share, hops = rows // poles, poles - 1
    widths = [columns * part // sum(PARTS) for part in PARTS]
    widest = max(widths)
    pairs1 = [(i ^ 1, i) for i in range(subs) if i ^ 1 < subs]
    pairs2 = [(j, i) for i in range(subs) for j in [((i + 1) ^ 1) - 1] if 0 <= j < subs]

    def exchange(one, two):
        one = lax.ppermute(one, "sub", pairs1)
        two = lax.ppermute(two, "sub", pairs2)
        return one, two

    one, two, sigma, sigma_share, order_row, *sources = call(
        functools.partial(start_kernel, rim),
        [((rim, columns), BF16), ((rim, columns), BF16), ((rows, widest), F32), ((share, widest), F32), ((1, order), F32)]
        + [((rows, n), F32) for n in widths],
        [(VMEM, conductivity), (VMEM, order_list), (VMEM, state)], moved=8 * rows * columns,
    )
    first_halo = exchange(one, two)
    (g_outer,) = call(
        setup_kernel, [((8 * rim, order), BF16)], [(VMEM, order_row), (VMEM, inverse)],
        flops=16 * rim * order * order, moved=6 * rows * order,
    )
    (g,) = call(
        inner_kernel, [((2 * rows, order), BF16)], [(VMEM, order_row), (VMEM, inverse), (VMEM, g_outer)],
        flops=4 * rows * order * order, moved=6 * rows * order,
    )

    def sweep(source, got, lane, tag, split):
        n = source.shape[1]
        ext, x, r, msgs = call(
            functools.partial(edge_kernel, rim, lane),
            [((order, n), BF16), ((2, rows + 16, n), F32), ((2, 2, rim, n), F32), ((2, 4 * rim + TAIL, n), F32)],
            [(SMEM, pole_shift), (VMEM, g_outer if tag == "00" else g), (VMEM, source), (VMEM, got[0]), (VMEM, got[1]), (VMEM, sigma)],
            flops=16 * rim * order * n, moved=4 * rows * order,
        )
        got = exchange(msgs[0].astype(F16), msgs[1].astype(F16))
        shares = [((share, n), F32)] + [((share + TAIL, n), F32)] * hops
        if not split:
            return call(
                functools.partial(tail_kernel, rim, hops), shares + [((2, rows + 16, n), F32)],
                [(SMEM, pole_shift), (SMEM, pole_weight), (VMEM, g), (VMEM, source), (VMEM, ext), (VMEM, x),
                 (VMEM, sigma), (VMEM, r), (VMEM, jnp.stack(got).astype(F32))],
                [pltpu.VMEM((rows, n), F32), pltpu.VMEM((2, order, n), BF16)],
                flops=8 * rows * order * n, moved=4 * rows * order, alias={5: 1 + hops},
            )[:-1]
        part, x = call(
            functools.partial(middle_kernel, rim), [((rows, n), F32), ((2, rows + 16, n), F32)],
            [(SMEM, pole_shift), (SMEM, pole_weight), (VMEM, g), (VMEM, source), (VMEM, ext), (VMEM, x), (VMEM, sigma)],
            [pltpu.VMEM((2, rows - 2 * rim, n), BF16)],
            flops=8 * rows * rows * n, moved=4 * rows * order, alias={5: 1},
        )
        return call(
            functools.partial(last_kernel, rim, hops), shares,
            [(SMEM, pole_weight), (VMEM, g), (VMEM, part), (VMEM, x), (VMEM, r), (VMEM, jnp.stack(got).astype(F32))],
            [pltpu.VMEM((rows, n), F32), pltpu.VMEM((2, 4 * rim, n), BF16)],
            flops=8 * rows * 4 * rim * n, moved=4 * rows * order,
        )

    def moved(sent):
        own, *sent = sent
        got = []
        for hop, block in enumerate(sent):
            got.append(lax.ppermute(block.astype(F16), "pole", hop_pairs(hop + 1, poles)))
        return [own] + [x.astype(F32) for x in got]

    def gathered(own):
        got, n = [], own.shape[1]
        for hop in range(hops):
            got.append(lax.ppermute(own, "pole", hop_pairs(hop + 1, poles)))
        return call(
            functools.partial(join_kernel, rim),
            [((rows, n), BF16), ((rim, n), BF16), ((rim, n), BF16)],
            [(VMEM, own)] + [(VMEM, x) for x in got], moved=4 * rows * n,
        )

    results, lane = [], 0
    for chunk, n in enumerate(widths):
        source, halo = sources[chunk], first_halo
        for step in range(STEPS):
            tag = f"{chunk}{step}"
            terms = moved(sweep(source, halo, 0 if step else lane, tag, split_at(chunk, step)))
            if step + 1 < STEPS:
                (total,) = call(
                    sum_kernel, [((share, n), BF16)], [(VMEM, x) for x in [sigma_share] + terms],
                    moved=4 * rows * n,
                )
                source, one, two = gathered(total)
                halo = exchange(one, two)
        results.extend(terms)
        lane += n
    return call(final_kernel, [((share, columns), F32)], [(VMEM, x) for x in results], moved=4 * rows * columns)[0]


def solution(mesh):
    placed = (
        P("sub", None),
        P("sub"),
        P("pole", None),
        P("pole", None),
        P("sub", None),
        P("pole", "sub", None),
    )
    return jax.shard_map(
        shards, mesh=mesh, in_specs=placed, out_specs=P(("sub", "pole"), None), check_vma=False
    )
```

```python
import functools

import jax
import jax.numpy as jnp
from jax import lax
from jax.experimental import pallas as pl
from jax.experimental.pallas import tpu as pltpu
from jax.sharding import PartitionSpec as P


STEPS = 2
PARTS = (1, 1)
TAIL = 8
TOP = 12.0
BF16 = jnp.bfloat16
F16 = jnp.float16
F32 = jnp.float32
VMEM = pl.BlockSpec(memory_space=pltpu.VMEM)
SMEM = pl.BlockSpec(memory_space=pltpu.SMEM)


def split_at(chunk, step):
    return chunk == 0 or step == 0


def call(kernel, outs, ins, scratch=(), flops=0, moved=0, alias=()):
    return pl.pallas_call(
        kernel,
        out_shape=[jax.ShapeDtypeStruct(s, d) for s, d in outs],
        in_specs=[s for s, _ in ins],
        out_specs=[VMEM] * len(outs),
        scratch_shapes=list(scratch),
        input_output_aliases=dict(alias),
        compiler_params=pltpu.CompilerParams(vmem_limit_bytes=16 * 2**20),
        cost_estimate=pl.CostEstimate(flops=flops, bytes_accessed=moved, transcendentals=0),
    )(*[a for _, a in ins])


def dot(a, b):
    return jnp.dot(a, b, preferred_element_type=F32)


def store_coded(ref, blocks):
    top = functools.reduce(jnp.maximum, [jnp.max(jnp.abs(b), axis=0, keepdims=True) for b in blocks])
    power = jnp.ceil(jnp.log2(jnp.maximum(top, 1e-30)))
    scale, at = jnp.exp2(TOP - power), 0
    for block in blocks:
        ref[at:at + block.shape[0]] = block * scale
        at += block.shape[0]
    ref[at:] = jnp.broadcast_to(power, (TAIL, top.shape[1]))


def pick(flag, a, b):
    return jnp.where(flag == 0, a, b)


def hop_target(pole, hop, poles):
    return pole ^ hop if poles & (poles - 1) == 0 else lax.rem(pole + hop, poles)


def hop_source(pole, hop, poles):
    return pole ^ hop if poles & (poles - 1) == 0 else lax.rem(pole + poles - hop, poles)


def hop_pairs(hop, poles):
    return [(i, i ^ hop if poles & (poles - 1) == 0 else (i + hop) % poles) for i in range(poles)]


def rows_of(index, share):
    return pl.ds(pl.multiple_of(index * share, share), share)


def column(row, count):
    return jnp.transpose(jnp.broadcast_to(row, (8, count)))[:, :1]


def start_kernel(rim, packed_ref, state_ref, msg1_ref, msg2_ref, wide_ref, share_ref, row_ref, *chunks):
    rows, share, lane = state_ref.shape[0], share_ref.shape[0], 0
    parity = lax.rem(lax.axis_index("sub"), 2)
    sigma = column(packed_ref[:, :rows], rows)
    low = (state_ref[:rim] * sigma[:rim]).astype(BF16)
    high = (state_ref[rows - rim:] * sigma[rows - rim:]).astype(BF16)
    msg1_ref[...] = pick(parity, high, low)
    msg2_ref[...] = pick(parity, low, high)
    wide_ref[...] = jnp.broadcast_to(sigma, wide_ref.shape)
    share_ref[...] = wide_ref[rows_of(lax.axis_index("pole"), share)]
    row_ref[...] = packed_ref[:, rows:]
    for ref in chunks:
        ref[...] = state_ref[:, lane:lane + ref.shape[1]] * sigma
        lane += ref.shape[1]


def places(row_ref):
    width = row_ref.shape[1]
    ids = lax.broadcasted_iota(jnp.int32, (width, width), 1)
    return (column(row_ref[...], width).astype(jnp.int32) == ids).astype(BF16)


def setup_kernel(row_ref, inv_ref, outer_ref):
    rows, width = inv_ref.shape[1], row_ref.shape[1]
    span, place = outer_ref.shape[0] // 4, places(row_ref)
    for half in range(2):
        part = inv_ref.at[0, :, half * width:(half + 1) * width]
        for side, lo in ((0, 0), (1, rows - span)):
            at = (2 * half + side) * span
            outer_ref[at:at + span] = dot(part[lo:lo + span], place).astype(BF16)


def inner_kernel(row_ref, inv_ref, outer_ref, g_ref):
    rows, width = inv_ref.shape[1], row_ref.shape[1]
    span, place = outer_ref.shape[0] // 4, places(row_ref)
    for half in range(2):
        part = inv_ref.at[0, :, half * width:(half + 1) * width]
        for side, lo in ((0, 0), (1, rows - span)):
            at = (2 * half + side) * span
            g_ref[half * rows + lo:half * rows + lo + span] = outer_ref[at:at + span]
        if rows > 2 * span:
            g_ref[half * rows + span:(half + 1) * rows - span] = dot(part[span:rows - span], place).astype(BF16)


def stencil(x_ref, half, lo, count, rim, far_up, far_down):
    def row(shift):
        return x_ref[half, 8 + lo + shift:8 + lo + shift + count]

    mid = 4.0 * row(0) - row(-1) - row(1)
    if far_up:
        mid = mid - row(-rim)
    if far_down:
        mid = mid - row(rim)
    return mid


def residual(x_ref, lo, count, rim, far_up, far_down, src_ref, sigma_ref, a, b):
    at = slice(lo, lo + count)
    xr, xi = x_ref[0, 8 + lo:8 + lo + count], x_ref[1, 8 + lo:8 + lo + count]
    sigma = sigma_ref[at, :src_ref.shape[1]]
    real = src_ref[at].astype(F32) - stencil(x_ref, 0, lo, count, rim, far_up, far_down) - sigma * (a * xr - b * xi)
    imag = -stencil(x_ref, 1, lo, count, rim, far_up, far_down) - sigma * (b * xr + a * xi)
    return real, imag


def edge_kernel(rim, lane, shift_ref, g_ref, src_ref, one_ref, two_ref, sigma_ref, ext_ref, x_ref, r_ref, msgs_ref):
    rows, n = src_ref.shape
    parity = lax.rem(lax.axis_index("sub"), 2)
    one, two = one_ref[:, lane:lane + n], two_ref[:, lane:lane + n]
    ext_ref[:rim] = pick(parity, two, one)
    ext_ref[rim:rim + rows] = src_ref[...].astype(BF16)
    ext_ref[rim + rows:] = pick(parity, one, two)
    a, b = shift_ref[0, 0], shift_ref[0, 1]
    span, step = 2 * rim, 32
    x_ref[:, :8] = jnp.zeros((2, 8, n), F32)
    x_ref[:, 8 + rows:] = jnp.zeros((2, 8, n), F32)
    for lo in (0, rows - span):
        for half in range(2):
            at = half * rows + lo if g_ref.shape[0] == 2 * rows else (2 * half + (lo > 0)) * span
            x_ref[half, 8 + lo:8 + lo + span] = dot(g_ref[at:at + span], ext_ref[...])
    for side, lo in ((0, 0), (1, rows - rim)):
        for k in range(0, rim, step):
            out = residual(x_ref, lo + k, step, rim, side == 1, side == 0, src_ref, sigma_ref, a, b)
            for half in range(2):
                r_ref[side, half, k:k + step] = out[half]
        blocks = [x_ref[half, 8 + lo:8 + lo + rim] for half in range(2)] + [r_ref[side, half] for half in range(2)]
        store_coded(msgs_ref.at[parity if side else 1 - parity], blocks)


def add_product(rows, g_ref, cols, er, ei, wr, wi, base, out_ref):
    block = rows // 3 if rows % 384 == 0 else rows
    for lo in range(0, rows, block):
        gr, gi = [jnp.concatenate([g_ref[half + lo:half + lo + block, c] for c in cols], axis=1) for half in (0, rows)]
        real = dot(gr, er) - dot(gi, ei)
        imag = dot(gr, ei) + dot(gi, er)
        out_ref[lo:lo + block] = base(lo, block) + (wr * real - wi * imag)


def inner_residual(rim, shift_ref, g_ref, src_ref, ext_ref, sigma_ref, x_ref, e_ref, at):
    rows = src_ref.shape[0]
    span, step = 2 * rim, 32
    a, b = shift_ref[0, 0], shift_ref[0, 1]
    if rows > 2 * span:
        for half in range(2):
            x_ref[half, 8 + span:8 + rows - span] = dot(g_ref[half * rows + span:(half + 1) * rows - span], ext_ref[...])
    for lo in range(rim, rows - rim, step):
        out = residual(x_ref, lo, step, rim, True, True, src_ref, sigma_ref, a, b)
        for half in range(2):
            e_ref[half, at + lo - rim:at + lo - rim + step] = out[half].astype(BF16)


def outer_residual(rim, x_ref, r_ref, got_ref, e_ref, after_at):
    rows = x_ref.shape[1] - 16
    sub = lax.axis_index("sub")
    parity = lax.rem(sub, 2)
    before_ref, after_ref = got_ref.at[1 - parity], got_ref.at[parity]
    inner_up = jnp.where(sub == 0, 0.0, 1.0)
    inner_down = jnp.where(sub == lax.axis_size("sub") - 1, 0.0, 1.0)
    up_scale = jnp.exp2(before_ref[4 * rim:4 * rim + 1] - TOP)
    down_scale = jnp.exp2(after_ref[4 * rim:4 * rim + 1] - TOP)
    at = lax.broadcasted_iota(jnp.int32, (rim, 1), 0)
    for half in range(2):
        x, r = slice(half * rim, (half + 1) * rim), slice((2 + half) * rim, (3 + half) * rim)
        xb, qb = before_ref[x] * up_scale, before_ref[r] * up_scale
        xa, qa = after_ref[x] * down_scale, after_ref[r] * down_scale
        low, high = x_ref[half, 8:8 + rim], x_ref[half, 8 + rows - rim:8 + rows]
        above = qb + low + jnp.where(at == rim - 1, low[:1], 0.0)
        below = qa + high + jnp.where(at == 0, high[rim - 1:], 0.0)
        head = r_ref[0, half] + xb + jnp.where(at == 0, xb[rim - 1:], 0.0)
        foot = r_ref[1, half] + xa + jnp.where(at == rim - 1, xa[:1], 0.0)
        e_ref[half, :rim] = (inner_up * above).astype(BF16)
        e_ref[half, rim:2 * rim] = head.astype(BF16)
        e_ref[half, after_at:after_at + rim] = foot.astype(BF16)
        e_ref[half, after_at + rim:after_at + 2 * rim] = (inner_down * below).astype(BF16)


def store_shares(u_ref, own_ref, msgs):
    share, poles, pole = own_ref.shape[0], len(msgs) + 1, lax.axis_index("pole")
    own_ref[...] = u_ref[rows_of(pole, share)]
    for hop, ref in enumerate(msgs):
        store_coded(ref, [u_ref[rows_of(hop_target(pole, hop + 1, poles), share)]])


def middle_kernel(rim, shift_ref, weight_ref, g_ref, src_ref, ext_ref, outer_ref, sigma_ref, out_ref, x_ref, e_ref):
    rows, _ = src_ref.shape
    wr, wi = 2.0 * weight_ref[0, 0], 2.0 * weight_ref[0, 1]
    inner_residual(rim, shift_ref, g_ref, src_ref, ext_ref, sigma_ref, x_ref, e_ref, 0)

    def base(lo, count):
        return wr * x_ref[0, 8 + lo:8 + lo + count] - wi * x_ref[1, 8 + lo:8 + lo + count]

    add_product(rows, g_ref, [slice(2 * rim, rows)], e_ref[0], e_ref[1], wr, wi, base, out_ref)


def last_kernel(rim, hops, weight_ref, g_ref, part_ref, x_ref, r_ref, got_ref, *rest):
    own_ref, msgs, u_ref, e_ref = rest[0], rest[1:1 + hops], rest[1 + hops], rest[2 + hops]
    rows, _ = part_ref.shape
    wr, wi = 2.0 * weight_ref[0, 0], 2.0 * weight_ref[0, 1]
    outer_residual(rim, x_ref, r_ref, got_ref, e_ref, rim * 2)
    add_product(
        rows, g_ref, [slice(0, 2 * rim), slice(rows, rows + 2 * rim)], e_ref[0], e_ref[1], wr, wi,
        lambda lo, count: part_ref[lo:lo + count], u_ref,
    )
    store_shares(u_ref, own_ref, msgs)


def tail_kernel(rim, hops, shift_ref, weight_ref, g_ref, src_ref, ext_ref, outer_ref, sigma_ref, r_ref, got_ref, *rest):
    own_ref, msgs, x_ref, u_ref, e_ref = rest[0], rest[1:1 + hops], rest[1 + hops], rest[2 + hops], rest[3 + hops]
    rows, _ = src_ref.shape
    span = 2 * rim
    wr, wi = 2.0 * weight_ref[0, 0], 2.0 * weight_ref[0, 1]
    inner_residual(rim, shift_ref, g_ref, src_ref, ext_ref, sigma_ref, x_ref, e_ref, span)
    outer_residual(rim, x_ref, r_ref, got_ref, e_ref, rows)

    def base(lo, count):
        return wr * x_ref[0, 8 + lo:8 + lo + count] - wi * x_ref[1, 8 + lo:8 + lo + count]

    add_product(rows, g_ref, [slice(0, rows + span)], e_ref[0], e_ref[1], wr, wi, base, u_ref)
    store_shares(u_ref, own_ref, msgs)


def summed(own_ref, got):
    share = own_ref.shape[0]
    total = own_ref[...]
    for ref in got:
        total = total + ref[:share] * jnp.exp2(ref[share:share + 1] - TOP)
    return total


def sum_kernel(factor_ref, own_ref, *rest):
    got, total_ref = rest[:-1], rest[-1]
    total_ref[...] = (summed(own_ref, got) * factor_ref[:, :total_ref.shape[1]]).astype(BF16)


def final_kernel(*refs):
    sets, out_ref, lane = refs[:-1], refs[-1], 0
    each = len(sets) // len(PARTS)
    for at in range(0, len(sets), each):
        n = sets[at].shape[1]
        out_ref[:, lane:lane + n] = summed(sets[at], sets[at + 1:at + each])
        lane += n


def join_kernel(rim, own_ref, *rest):
    got, (src_ref, msg1_ref, msg2_ref) = rest[:-3], rest[-3:]
    share, rows, poles = own_ref.shape[0], src_ref.shape[0], len(got) + 1
    parity, pole = lax.rem(lax.axis_index("sub"), 2), lax.axis_index("pole")
    src_ref[rows_of(pole, share)] = own_ref[...]
    for hop, ref in enumerate(got):
        src_ref[rows_of(hop_source(pole, hop + 1, poles), share)] = ref[...]
    low, high = src_ref[:rim], src_ref[rows - rim:]
    msg1_ref[...] = pick(parity, high, low)
    msg2_ref[...] = pick(parity, low, high)


def shards(state, conductivity, pole_shift, pole_weight, order_list, inverse):
    rows, columns = state.shape
    order = order_list.shape[1]
    rim = (order - rows) // 2
    subs, poles = lax.axis_size("sub"), lax.axis_size("pole")
    share, hops = rows // poles, poles - 1
    widths = [columns * part // sum(PARTS) for part in PARTS]
    widest = max(widths)
    pairs1 = [(i ^ 1, i) for i in range(subs) if i ^ 1 < subs]
    pairs2 = [(j, i) for i in range(subs) for j in [((i + 1) ^ 1) - 1] if 0 <= j < subs]

    def exchange(one, two):
        one = lax.ppermute(one, "sub", pairs1)
        two = lax.ppermute(two, "sub", pairs2)
        return one, two

    packed = jnp.concatenate([conductivity, order_list[0].astype(F32)])[None]
    one, two, sigma, sigma_share, order_row, *sources = call(
        functools.partial(start_kernel, rim),
        [((rim, columns), BF16), ((rim, columns), BF16), ((rows, widest), F32), ((share, widest), F32), ((1, order), F32)]
        + [((rows, n), F32) for n in widths],
        [(VMEM, packed), (VMEM, state)], moved=8 * rows * columns,
    )
    first_halo = exchange(one, two)
    (g_outer,) = call(
        setup_kernel, [((8 * rim, order), BF16)], [(VMEM, order_row), (VMEM, inverse)],
        flops=16 * rim * order * order, moved=6 * rows * order,
    )
    (g,) = call(
        inner_kernel, [((2 * rows, order), BF16)], [(VMEM, order_row), (VMEM, inverse), (VMEM, g_outer)],
        flops=4 * rows * order * order, moved=6 * rows * order,
    )

    def sweep(source, got, lane, tag, split):
        n = source.shape[1]
        ext, x, r, msgs = call(
            functools.partial(edge_kernel, rim, lane),
            [((order, n), BF16), ((2, rows + 16, n), F32), ((2, 2, rim, n), F32), ((2, 4 * rim + TAIL, n), F32)],
            [(SMEM, pole_shift), (VMEM, g_outer if tag == "00" else g), (VMEM, source), (VMEM, got[0]), (VMEM, got[1]), (VMEM, sigma)],
            flops=16 * rim * order * n, moved=4 * rows * order,
        )
        got = exchange(msgs[0].astype(F16), msgs[1].astype(F16))
        shares = [((share, n), F32)] + [((share + TAIL, n), F32)] * hops
        if not split:
            return call(
                functools.partial(tail_kernel, rim, hops), shares + [((2, rows + 16, n), F32)],
                [(SMEM, pole_shift), (SMEM, pole_weight), (VMEM, g), (VMEM, source), (VMEM, ext), (VMEM, x),
                 (VMEM, sigma), (VMEM, r), (VMEM, jnp.stack(got).astype(F32))],
                [pltpu.VMEM((rows, n), F32), pltpu.VMEM((2, order, n), BF16)],
                flops=8 * rows * order * n, moved=4 * rows * order, alias={5: 1 + hops},
            )[:-1]
        part, x = call(
            functools.partial(middle_kernel, rim), [((rows, n), F32), ((2, rows + 16, n), F32)],
            [(SMEM, pole_shift), (SMEM, pole_weight), (VMEM, g), (VMEM, source), (VMEM, ext), (VMEM, x), (VMEM, sigma)],
            [pltpu.VMEM((2, rows - 2 * rim, n), BF16)],
            flops=8 * rows * rows * n, moved=4 * rows * order, alias={5: 1},
        )
        return call(
            functools.partial(last_kernel, rim, hops), shares,
            [(SMEM, pole_weight), (VMEM, g), (VMEM, part), (VMEM, x), (VMEM, r), (VMEM, jnp.stack(got).astype(F32))],
            [pltpu.VMEM((rows, n), F32), pltpu.VMEM((2, 4 * rim, n), BF16)],
            flops=8 * rows * 4 * rim * n, moved=4 * rows * order,
        )

    def moved(sent):
        own, *sent = sent
        got = []
        for hop, block in enumerate(sent):
            got.append(lax.ppermute(block.astype(F16), "pole", hop_pairs(hop + 1, poles)))
        return [own] + [x.astype(F32) for x in got]

    def gathered(own):
        got, n = [], own.shape[1]
        for hop in range(hops):
            got.append(lax.ppermute(own, "pole", hop_pairs(hop + 1, poles)))
        return call(
            functools.partial(join_kernel, rim),
            [((rows, n), BF16), ((rim, n), BF16), ((rim, n), BF16)],
            [(VMEM, own)] + [(VMEM, x) for x in got], moved=4 * rows * n,
        )

    results, lane = [], 0
    for chunk, n in enumerate(widths):
        source, halo = sources[chunk], first_halo
        for step in range(STEPS):
            tag = f"{chunk}{step}"
            terms = moved(sweep(source, halo, 0 if step else lane, tag, split_at(chunk, step)))
            if step + 1 < STEPS:
                (total,) = call(
                    sum_kernel, [((share, n), BF16)], [(VMEM, x) for x in [sigma_share] + terms],
                    moved=4 * rows * n,
                )
                source, one, two = gathered(total)
                halo = exchange(one, two)
        results.extend(terms)
        lane += n
    return call(final_kernel, [((share, columns), F32)], [(VMEM, x) for x in results], moved=4 * rows * columns)[0]


def solution(mesh):
    placed = (
        P("sub", None),
        P("sub"),
        P("pole", None),
        P("pole", None),
        P("sub", None),
        P("pole", "sub", None),
    )
    return jax.shard_map(
        shards, mesh=mesh, in_specs=placed, out_specs=P(("sub", "pole"), None), check_vma=False
    )
```
